512 devices in a mesh: rows: 8 (over z_lo, core), vec: 64 (over x, y, z_hi).
Axes of the slice: x: 4, y: 8, z: 8 (z_hi: 2, z_lo: 4; z = z_hi * 4 + z_lo), core: 2. Of those that a mesh axis runs over, the one named last changes fastest.
Arguments:
- vectors: float32 [512, 32768], P('vec', 'rows'), may hold values from -6 to 6
- tile_table: float32 [16, 128, 128], replicated, may hold values from -0.3125 to 0.3125
- offsets: int32 [256, 3], P('rows'), may hold values from -2 to 2, as said below
- tile_ids: int32 [256, 3], P('rows'), may hold values from 0 to 15
- bounds: float32 [3], replicated, may hold values from -1.9 to 2.3, as said below
Outputs:
- filtered: float32 [512, 32768], P('vec', 'rows')
- gram_matrix: float32 [512, 512], P(('rows', 'vec'))
The draws below stay inside these ranges and needn't reach their ends.
Inputs may be any that keep to these rules, and one draw needn't show every extreme that they name: offsets[j, 0] is 0 for every row block j; wherever offsets[j, s] = o is not 0 and j + o lies in 0..255, row block j + o has a slot with offset -o and the same tile number, so the Hamiltonian is symmetric. bounds[0] < bounds[1] < bounds[2]; bounds[1] - bounds[0] lies between 0.1 and 0.3, bounds[2] - bounds[1] between 3.0 and 3.6, and bounds[1] + bounds[2] between 0.4 and 1.0.
All inputs are finite; a program needn't handle non-finite values.
Results may differ from the reference program's by a relative error of at most 0.00013.
Values sent between devices are 32-bit elements; how exact they have to be, the bound alone decides.
No kernel may reach another device: no remote copies, remote signals or barrier semaphores. Data moves between devices by JAX's collectives and lax.ppermute only.
A program may use at most 64 MiB of HBM per device.

```python
import jax
import jax.numpy as jnp
from jax import lax

K = 512
BLOCK = 128
NB = 3
NT = 16
STEPS = 4
N = 32768
NBLK = 256


def matching(pattern, id_values):
    pair_offsets = jnp.array([2, 2, -2, -2], dtype=jnp.int32)
    near_offsets = jnp.array([0, 1, -1, 0], dtype=jnp.int32)
    first_id = id_values[:, 0]
    second_id = id_values[:, 1]
    pair_ids = jnp.stack([first_id, second_id, first_id, second_id], axis=1)
    near_ids = jnp.stack([id_values[:, 2], first_id, first_id, id_values[:, 3]], axis=1)
    use_pair = (pattern == 0)[:, None]
    return (jnp.where(use_pair, pair_offsets[None, :], near_offsets[None, :]).reshape(-1), jnp.where(use_pair, pair_ids, near_ids).reshape(-1))


def banded_structure(key):
    base = jax.random.fold_in(key, 29)
    subkeys = jax.random.split(base, 6)
    group_count = NBLK // 4
    pattern_one = jax.random.randint(subkeys[0], (group_count,), 0, 2, dtype=jnp.int32)
    pattern_two = jax.random.randint(subkeys[1], (group_count - 1,), 0, 2, dtype=jnp.int32)
    ids_one = jax.random.randint(subkeys[2], (group_count, 4), 0, NT, dtype=jnp.int32)
    ids_two = jax.random.randint(subkeys[3], (group_count - 1, 4), 0, NT, dtype=jnp.int32)
    diag_ids = jax.random.randint(subkeys[4], (NBLK,), 0, NT, dtype=jnp.int32)
    diag_ids = diag_ids.at[0].set(0).at[1].set(NT - 1)
    end_ids = jax.random.randint(subkeys[5], (4,), 0, NT, dtype=jnp.int32)
    offsets_one, tiles_one = matching(pattern_one, ids_one)
    inner_offsets, inner_tiles = matching(pattern_two, ids_two)
    low_end = jnp.array([-2, -2], dtype=jnp.int32)
    high_end = jnp.array([2, 2], dtype=jnp.int32)
    offsets_two = jnp.concatenate([low_end, inner_offsets, high_end])
    tiles_two = jnp.concatenate([end_ids[:2], inner_tiles, end_ids[2:]])
    offsets = jnp.stack([jnp.zeros((NBLK,), jnp.int32), offsets_one, offsets_two], axis=1)
    tile_ids = jnp.stack([diag_ids, tiles_one, tiles_two], axis=1)
    return (offsets.astype(jnp.int32), tile_ids.astype(jnp.int32))


def draw_offsets(key, part):
    return banded_structure(key)[0]


def draw_tile_ids(key, part):
    return banded_structure(key)[1]


def draw_bounds(key, part):
    subkeys = jax.random.split(jax.random.fold_in(key, 17), 3)
    centre = jax.random.uniform(subkeys[0], (), jnp.float32, 0.2, 0.5)
    half_width = jax.random.uniform(subkeys[1], (), jnp.float32, 1.5, 1.8)
    margin_gap = jax.random.uniform(subkeys[2], (), jnp.float32, 0.1, 0.3)
    return jnp.stack([centre - half_width - margin_gap, centre - half_width, centre + half_width]).astype(jnp.float32)


def levels(own_key, shape, shards, least, high):
    level = 1.0
    for axis_at, parts in shards:
        heights = jax.random.uniform(jax.random.fold_in(jax.random.fold_in(own_key, 6), axis_at), (parts,), jnp.float32, least / len(shards), high / len(shards))
        level = level * jnp.repeat(jnp.exp(heights), shape[axis_at] // parts).reshape((-1,) + (1,) * (len(shape) - 1 - axis_at))
    return level


def centred(key, extent, scale, limit, pieces=(), kind=jnp.bfloat16):
    values = scale * jax.random.normal(key, extent, jnp.float32)
    if pieces:
        values = values * levels(key, extent, pieces, -0.22, 0.18)
    return jnp.clip(values, -limit, limit).astype(kind)


def setup_inputs(seed: int = 0) -> dict:
    key_of = jax.random.split(jax.random.key(seed), 6)
    return {
        "vectors": centred(key_of[0], (K, N), 1.0, 6.0, ((0, 64), (1, 8)), jnp.float32),
        "tile_table": centred(key_of[1], (NT, BLOCK, BLOCK), (NB * BLOCK) ** -0.5, 0.3125, (), jnp.float32),
        "offsets": draw_offsets(jax.random.fold_in(key_of[5], 71), 0),
        "tile_ids": draw_tile_ids(jax.random.fold_in(key_of[5], 71), 0),
        "bounds": draw_bounds(jax.random.fold_in(key_of[5], 71), 0),
    }


def band_apply(blocks, tile_table, offsets, tile_ids):
    block_count = blocks.shape[0]
    flipped = tile_table.transpose(0, 2, 1)
    variants = jnp.concatenate([tile_table, flipped, (tile_table + flipped) / 2], axis=0)
    accumulated_total = jnp.zeros_like(blocks)
    block_index = jnp.arange(block_count, dtype=jnp.int32)
    for column in range(NB):
        shift = offsets[:, column].astype(jnp.int32)
        tile_kind = jnp.where(shift > 0, 0, jnp.where(shift < 0, 1, 2)).astype(jnp.int32)
        table_index = (tile_ids[:, column].astype(jnp.int32) + NT * tile_kind).astype(jnp.int32)
        source_block = (block_index + shift).astype(jnp.int32)
        inside = ((source_block >= 0) & (source_block < block_count)).astype(blocks.dtype)
        incoming_block = blocks[jnp.clip(source_block, 0, block_count - 1)] * inside[:, None, None]
        selected_entry = variants[table_index]
        accumulated_total = accumulated_total + jnp.einsum("swh,sqh->swq", incoming_block, selected_entry, precision=lax.Precision.HIGHEST)
    return accumulated_total


def reference(vectors, tile_table, offsets, tile_ids, bounds):
    blocks = vectors.reshape(K, NBLK, BLOCK).transpose(1, 0, 2)
    half_width = (bounds[2] - bounds[1]) / 2
    centre = (bounds[2] + bounds[1]) / 2
    sigma_one = half_width / (bounds[0] - centre)
    sigma_base = 2 / sigma_one
    previous = blocks
    present_vectors = (sigma_one / half_width) * (band_apply(blocks, tile_table, offsets, tile_ids) - centre * blocks)
    sigma_now = sigma_one
    for repeat in range(STEPS - 1):
        sigma_next = 1 / (sigma_base - sigma_now)
        advanced = (2 * sigma_next / half_width) * (band_apply(present_vectors, tile_table, offsets, tile_ids) - centre * present_vectors) - (sigma_now * sigma_next) * previous
        previous = present_vectors
        present_vectors = advanced
        sigma_now = sigma_next
    filtered = present_vectors.transpose(1, 0, 2).reshape(K, N)
    gram_matrix = jnp.dot(filtered, filtered.T, precision=lax.Precision.HIGHEST, preferred_element_type=jnp.float32) / N
    return filtered, gram_matrix
```

```python
import jax
import jax.numpy as jnp
from jax import lax
from jax.experimental import pallas as pl
from jax.experimental.pallas import tpu as pltpu
from jax.sharding import Mesh, PartitionSpec as P

BLOCK = 128
STEPS = 4
REACH = 2
HALO = STEPS * REACH
NT = 16
MIB = 1 << 20
ROWS = ("zl", "core")
VEC = ("x", "y", "zh")


def split(value):
    high = value.astype(jnp.bfloat16).astype(jnp.float32)
    return high, value - high


def table_kernel(tiles_ref, table_ref):
    for tile in range(NT):
        straight = tiles_ref[tile]
        flipped = straight.T
        for kind, matrix in enumerate((flipped, straight, (straight + flipped) / 2)):
            high, low = split(matrix)
            entry = tile + NT * kind
            table_ref[entry, :, :BLOCK] = high.astype(jnp.bfloat16)
            table_ref[entry, :, BLOCK:] = low.astype(jnp.bfloat16)


def filter_kernel(
    vectors_ref, before_ref, after_ref, own_ref, table_ref, bounds_ref,
    filtered_ref, outgoing_ref,
    field_a, field_b, field_c, parts_a, parts_b, plan_vector, plan, sem,
):
    vecs = vectors_ref.shape[0]
    count = vectors_ref.shape[1] // BLOCK
    extent = count + 2 * HALO
    edge = HALO * BLOCK

    lane = lax.broadcasted_iota(jnp.int32, (8, 128), 1)
    row = lax.broadcasted_iota(jnp.int32, (8, 128), 0)
    left = pltpu.roll(before_ref[:, edge:], 128 - (count - HALO), 1)
    own = pltpu.roll(own_ref[...], HALO, 1)
    right = pltpu.roll(after_ref[:, edge:], HALO + count, 1)
    meta = jnp.where(lane < HALO, left, jnp.where(lane < HALO + count, own, right))
    meta = meta.astype(jnp.int32)
    shift = pltpu.roll(meta, 3, 0)
    kind = jnp.where(shift > 0, 0, jnp.where(shift < 0, NT, 2 * NT))
    plan_vector[...] = jnp.where(row < 3, meta + lane, meta + kind)
    copy = pltpu.make_async_copy(plan_vector, plan, sem)
    copy.start()

    def store_parts(target, block, value):
        high, low = split(value)
        target[block] = jnp.concatenate([high, low], axis=0).astype(jnp.bfloat16)

    for block in range(extent):
        if block < HALO:
            value = before_ref[:, block * BLOCK : (block + 1) * BLOCK]
        elif block < HALO + count:
            at = (block - HALO) * BLOCK
            value = vectors_ref[:, at : at + BLOCK]
        else:
            at = (block - HALO - count) * BLOCK
            value = after_ref[:, at : at + BLOCK]
        field_a[block] = value
        store_parts(parts_a, block, value)

    lowest, low_end, high_end = bounds_ref[0], bounds_ref[1], bounds_ref[2]

    def spread(value):
        return jnp.full((vecs, BLOCK), value, jnp.float32)

    half_width = spread((high_end - low_end) * 0.5)
    centre = spread((high_end + low_end) * 0.5)
    sigma_one = half_width / (spread(lowest) - centre)
    sigma_base = 2 / sigma_one
    copy.wait()

    def product(parts, block):
        left_parts, right_parts = [], []
        for slot in range(3):
            left_parts.append(parts[plan[slot, block]])
            right_parts.append(table_ref[plan[3 + slot, block]])
        both = lax.dot_general(
            jnp.concatenate(left_parts, axis=1),
            jnp.concatenate(right_parts, axis=0),
            (((1,), (0,)), ((), ())),
            preferred_element_type=jnp.float32,
        )
        return both[:vecs, :BLOCK] + both[vecs:, :BLOCK] + both[:vecs, BLOCK:]

    fields = [field_a, field_b, field_c, field_a]
    parts = [parts_a, parts_b, parts_a, parts_b]
    sigma = sigma_one
    for step in range(1, STEPS + 1):
        source, source_parts = fields[step - 1], parts[step - 1]
        if step == 1:
            scale, drag = sigma_one / half_width, None
        else:
            following = 1 / (sigma_base - sigma)
            scale, drag = 2 * following / half_width, sigma * following
            sigma = following
        first = REACH * step

        def one_block(block):
            value = scale * (product(source_parts, block) - centre * source[block])
            if drag is not None:
                value = value - drag * fields[step - 2][block]
            if step < STEPS:
                fields[step][block] = value
                store_parts(parts[step], block, value)
            else:
                at = block - HALO
                filtered_ref[:, pl.ds(pl.multiple_of(at * BLOCK, BLOCK), BLOCK)] = value
                owner, part = at // 2, at % 2
                for copy_at in range(4):
                    outgoing_ref[
                        copy_at * (count // 2) + owner,
                        :,
                        pl.ds(pl.multiple_of(part * BLOCK, BLOCK), BLOCK),
                    ] = value

        group = 4

        @pl.loop(0, (extent - 2 * first) // group)
        def _(index):
            for inner in range(group):
                one_block(first + index * group + inner)


def gram_kernel(group_ref, stacked_ref, partial_ref, own_high, own_low):
    total = stacked_ref.shape[0]
    group = group_ref[0]
    high, low = split(stacked_ref[...])
    high, low = high.astype(jnp.bfloat16), low.astype(jnp.bfloat16)
    for part in range(8):
        rows = stacked_ref[pl.ds(pl.multiple_of(part * 64 + group * 16, 16), 16), :]
        own, rest = split(rows)
        own_high[part * 16 : (part + 1) * 16, :] = own.astype(jnp.bfloat16)
        own_low[part * 16 : (part + 1) * 16, :] = rest.astype(jnp.bfloat16)
    contract = (((1,), (1,)), ((), ()))

    def multiply(one, other):
        return lax.dot_general(one, other, contract, preferred_element_type=jnp.float32)

    a_high, a_low = own_high[...], own_low[...]
    partial = multiply(a_high, high) + multiply(a_high, low) + multiply(a_low, high)
    count = partial.shape[0]
    pieces = total // BLOCK
    for piece in range(pieces):
        partial_ref[pl.ds(piece, count, stride=pieces), :] = partial[
            :, piece * BLOCK : (piece + 1) * BLOCK
        ]


def on_device(vectors, tile_table, offsets, tile_ids, bounds):
    vecs, local_rows = vectors.shape
    count = local_rows // BLOCK
    extent = count + 2 * HALO
    edge = HALO * BLOCK
    meta = jnp.concatenate([offsets.T, tile_ids.T], axis=0).astype(jnp.float32)
    meta = jnp.pad(meta, ((0, 2), (0, BLOCK - count)))
    size = lax.axis_size(ROWS)
    up = [(i, i + 1) for i in range(size - 1)]
    down = [(j, i) for i, j in up]
    before = lax.ppermute(
        jnp.concatenate([vectors[:, local_rows - edge :], meta], axis=1), ROWS, up
    )
    after = lax.ppermute(jnp.concatenate([vectors[:, :edge], meta], axis=1), ROWS, down)

    vmem = pl.BlockSpec(memory_space=pltpu.VMEM)
    smem = pl.BlockSpec(memory_space=pltpu.SMEM)
    table = pl.pallas_call(
        table_kernel,
        out_shape=jax.ShapeDtypeStruct((3 * NT, BLOCK, 2 * BLOCK), jnp.bfloat16),
        in_specs=[vmem],
        out_specs=vmem,
        compiler_params=pltpu.CompilerParams(vmem_limit_bytes=16 * MIB),
        name="table",
    )(tile_table)

    field = pltpu.VMEM((extent, vecs, BLOCK), jnp.float32)
    parts = pltpu.VMEM((extent, 2 * vecs, BLOCK), jnp.bfloat16)
    filtered, outgoing = pl.pallas_call(
        filter_kernel,
        out_shape=(
            jax.ShapeDtypeStruct((vecs, local_rows), jnp.float32),
            jax.ShapeDtypeStruct((64, vecs, 2 * BLOCK), jnp.float32),
        ),
        in_specs=[vmem, vmem, vmem, vmem, vmem, smem],
        out_specs=(vmem, vmem),
        scratch_shapes=[
            field, field, field, parts, parts,
            pltpu.VMEM((8, BLOCK), jnp.int32),
            pltpu.SMEM((8, BLOCK), jnp.int32),
            pltpu.SemaphoreType.DMA(()),
        ],
        compiler_params=pltpu.CompilerParams(vmem_limit_bytes=16 * MIB),
        name="filter",
    )(vectors, before, after, meta, table, bounds)

    stacked = lax.all_to_all(outgoing, VEC, split_axis=0, concat_axis=0, tiled=True)
    total = 64 * vecs
    stacked = stacked.reshape(total, 2 * BLOCK)
    group = lax.axis_index("x").astype(jnp.int32).reshape(1)
    owned = total // 4
    partial = pl.pallas_call(
        gram_kernel,
        out_shape=jax.ShapeDtypeStruct((owned * (total // BLOCK), BLOCK), jnp.float32),
        in_specs=[smem, vmem],
        out_specs=vmem,
        scratch_shapes=[pltpu.VMEM((owned, 2 * BLOCK), jnp.bfloat16)] * 2,
        compiler_params=pltpu.CompilerParams(vmem_limit_bytes=16 * MIB),
        name="gram",
    )(group, stacked)
    received = lax.all_to_all(
        partial.reshape(owned, 1, total),
        ROWS + ("y", "zh"),
        split_axis=0,
        concat_axis=0,
        tiled=True,
    )
    gram_matrix = jnp.sum(received, axis=0) / (local_rows * size)
    return filtered, gram_matrix


def solution(mesh):
    fine = Mesh(mesh.devices.reshape(4, 2, 4, 8, 2), ROWS + VEC)
    placed = (P(VEC, ROWS), P(), P(ROWS, None), P(ROWS, None), P())
    return jax.shard_map(
        on_device,
        mesh=fine,
        in_specs=placed,
        out_specs=(P(VEC, ROWS), P(ROWS + VEC, None)),
        check_vma=False,
    )
```

```python
import jax
import jax.numpy as jnp
from jax import lax
from jax.experimental import pallas as pl
from jax.experimental.pallas import tpu as pltpu
from jax.sharding import Mesh, PartitionSpec as P

BLOCK = 128
STEPS = 4
REACH = 2
HALO = STEPS * REACH
NT = 16
MIB = 1 << 20
ROWS = ("zl", "core")
VEC = ("x", "y", "zh")


def split(value):
    high = value.astype(jnp.bfloat16).astype(jnp.float32)
    return high, value - high


def table_kernel(tiles_ref, table_ref):
    for tile in range(NT):
        straight = tiles_ref[tile]
        flipped = straight.T
        for kind, matrix in enumerate((flipped, straight, (straight + flipped) / 2)):
            high, low = split(matrix)
            entry = tile + NT * kind
            table_ref[entry, :, :BLOCK] = high.astype(jnp.bfloat16)
            table_ref[entry, :, BLOCK:] = low.astype(jnp.bfloat16)


def filter_kernel(
    vectors_ref, before_ref, after_ref, own_ref, table_ref, bounds_ref,
    filtered_ref, outgoing_ref,
    field_a, field_b, field_c, parts_a, parts_b, plan_vector, plan, sem,
):
    vecs = vectors_ref.shape[0]
    count = vectors_ref.shape[1] // BLOCK
    extent = count + 2 * HALO
    edge = HALO * BLOCK

    lane = lax.broadcasted_iota(jnp.int32, (8, 128), 1)
    row = lax.broadcasted_iota(jnp.int32, (8, 128), 0)
    left = pltpu.roll(before_ref[:, edge:], 128 - (count - HALO), 1)
    own = pltpu.roll(own_ref[...], HALO, 1)
    right = pltpu.roll(after_ref[:, edge:], HALO + count, 1)
    meta = jnp.where(lane < HALO, left, jnp.where(lane < HALO + count, own, right))
    meta = meta.astype(jnp.int32)
    shift = pltpu.roll(meta, 3, 0)
    kind = jnp.where(shift > 0, 0, jnp.where(shift < 0, NT, 2 * NT))
    plan_vector[...] = jnp.where(row < 3, meta + lane, meta + kind)
    copy = pltpu.make_async_copy(plan_vector, plan, sem)
    copy.start()

    def store_parts(target, block, value):
        high, low = split(value)
        target[block] = jnp.concatenate([high, low], axis=0).astype(jnp.bfloat16)

    for block in range(extent):
        if block < HALO:
            value = before_ref[:, block * BLOCK : (block + 1) * BLOCK]
        elif block < HALO + count:
            at = (block - HALO) * BLOCK
            value = vectors_ref[:, at : at + BLOCK]
        else:
            at = (block - HALO - count) * BLOCK
            value = after_ref[:, at : at + BLOCK]
        field_a[block] = value
        store_parts(parts_a, block, value)

    lowest, low_end, high_end = bounds_ref[0], bounds_ref[1], bounds_ref[2]

    def spread(value):
        return jnp.full((vecs, BLOCK), value, jnp.float32)

    half_width = spread((high_end - low_end) * 0.5)
    centre = spread((high_end + low_end) * 0.5)
    sigma_one = half_width / (spread(lowest) - centre)
    sigma_base = 2 / sigma_one
    copy.wait()

    def product(parts, block):
        left_parts, right_parts = [], []
        for slot in range(3):
            left_parts.append(parts[plan[slot, block]])
            right_parts.append(table_ref[plan[3 + slot, block]])
        both = lax.dot_general(
            jnp.concatenate(left_parts, axis=1),
            jnp.concatenate(right_parts, axis=0),
            (((1,), (0,)), ((), ())),
            preferred_element_type=jnp.float32,
        )
        return both[:vecs, :BLOCK] + both[vecs:, :BLOCK] + both[:vecs, BLOCK:]

    fields = [field_a, field_b, field_c, field_a]
    parts = [parts_a, parts_b, parts_a, parts_b]
    sigma = sigma_one
    for step in range(1, STEPS + 1):
        source, source_parts = fields[step - 1], parts[step - 1]
        if step == 1:
            scale, drag = sigma_one / half_width, None
        else:
            following = 1 / (sigma_base - sigma)
            scale, drag = 2 * following / half_width, sigma * following
            sigma = following
        first = REACH * step

        def one_block(block):
            value = scale * (product(source_parts, block) - centre * source[block])
            if drag is not None:
                value = value - drag * fields[step - 2][block]
            if step < STEPS:
                fields[step][block] = value
                store_parts(parts[step], block, value)
            else:
                at = block - HALO
                filtered_ref[:, pl.ds(pl.multiple_of(at * BLOCK, BLOCK), BLOCK)] = value
                owner, part = at // 2, at % 2
                for copy_at in range(4):
                    outgoing_ref[
                        copy_at * (count // 2) + owner,
                        :,
                        pl.ds(pl.multiple_of(part * BLOCK, BLOCK), BLOCK),
                    ] = value

        group = 4

        @pl.loop(0, (extent - 2 * first) // group)
        def _(index):
            for inner in range(group):
                one_block(first + index * group + inner)


def gram_kernel(stacked_ref, partial_ref, own_high, own_low):
    total = stacked_ref.shape[0]
    group = lax.axis_index("x")
    high, low = split(stacked_ref[...])
    high, low = high.astype(jnp.bfloat16), low.astype(jnp.bfloat16)
    for part in range(8):
        rows = stacked_ref[pl.ds(pl.multiple_of(part * 64 + group * 16, 16), 16), :]
        own, rest = split(rows)
        own_high[part * 16 : (part + 1) * 16, :] = own.astype(jnp.bfloat16)
        own_low[part * 16 : (part + 1) * 16, :] = rest.astype(jnp.bfloat16)
    contract = (((1,), (1,)), ((), ()))

    def multiply(one, other):
        return lax.dot_general(one, other, contract, preferred_element_type=jnp.float32)

    a_high, a_low = own_high[...], own_low[...]
    partial = multiply(a_high, high) + multiply(a_high, low) + multiply(a_low, high)
    count = partial.shape[0]
    pieces = total // BLOCK
    for piece in range(pieces):
        partial_ref[pl.ds(piece, count, stride=pieces), :] = partial[
            :, piece * BLOCK : (piece + 1) * BLOCK
        ]


def on_device(vectors, tile_table, offsets, tile_ids, bounds):
    vecs, local_rows = vectors.shape
    count = local_rows // BLOCK
    extent = count + 2 * HALO
    edge = HALO * BLOCK
    meta = jnp.concatenate([offsets.T, tile_ids.T], axis=0).astype(jnp.float32)
    meta = jnp.pad(meta, ((0, 2), (0, BLOCK - count)))
    size = lax.axis_size(ROWS)
    up = [(i, i + 1) for i in range(size - 1)]
    down = [(j, i) for i, j in up]
    before = lax.ppermute(
        jnp.concatenate([vectors[:, local_rows - edge :], meta], axis=1), ROWS, up
    )
    after = lax.ppermute(jnp.concatenate([vectors[:, :edge], meta], axis=1), ROWS, down)

    vmem = pl.BlockSpec(memory_space=pltpu.VMEM)
    smem = pl.BlockSpec(memory_space=pltpu.SMEM)
    table = pl.pallas_call(
        table_kernel,
        out_shape=jax.ShapeDtypeStruct((3 * NT, BLOCK, 2 * BLOCK), jnp.bfloat16),
        in_specs=[vmem],
        out_specs=vmem,
        compiler_params=pltpu.CompilerParams(vmem_limit_bytes=16 * MIB),
        name="table",
    )(tile_table)

    field = pltpu.VMEM((extent, vecs, BLOCK), jnp.float32)
    parts = pltpu.VMEM((extent, 2 * vecs, BLOCK), jnp.bfloat16)
    filtered, outgoing = pl.pallas_call(
        filter_kernel,
        out_shape=(
            jax.ShapeDtypeStruct((vecs, local_rows), jnp.float32),
            jax.ShapeDtypeStruct((64, vecs, 2 * BLOCK), jnp.float32),
        ),
        in_specs=[vmem, vmem, vmem, vmem, vmem, smem],
        out_specs=(vmem, vmem),
        scratch_shapes=[
            field, field, field, parts, parts,
            pltpu.VMEM((8, BLOCK), jnp.int32),
            pltpu.SMEM((8, BLOCK), jnp.int32),
            pltpu.SemaphoreType.DMA(()),
        ],
        compiler_params=pltpu.CompilerParams(vmem_limit_bytes=16 * MIB),
        name="filter",
    )(vectors, before, after, meta, table, bounds)

    stacked = lax.all_to_all(outgoing, VEC, split_axis=0, concat_axis=0, tiled=True)
    total = 64 * vecs
    stacked = stacked.reshape(total, 2 * BLOCK)
    owned = total // 4
    partial = pl.pallas_call(
        gram_kernel,
        out_shape=jax.ShapeDtypeStruct((owned * (total // BLOCK), BLOCK), jnp.float32),
        in_specs=[vmem],
        out_specs=vmem,
        scratch_shapes=[pltpu.VMEM((owned, 2 * BLOCK), jnp.bfloat16)] * 2,
        compiler_params=pltpu.CompilerParams(vmem_limit_bytes=16 * MIB),
        name="gram",
    )(stacked)
    received = lax.all_to_all(
        partial.reshape(owned, 1, total),
        ROWS + ("y", "zh"),
        split_axis=0,
        concat_axis=0,
        tiled=True,
    )
    gram_matrix = jnp.sum(received, axis=0) / (local_rows * size)
    return filtered, gram_matrix


def solution(mesh):
    fine = Mesh(mesh.devices.reshape(4, 2, 4, 8, 2), ROWS + VEC)
    placed = (P(VEC, ROWS), P(), P(ROWS, None), P(ROWS, None), P())
    return jax.shard_map(
        on_device,
        mesh=fine,
        in_specs=placed,
        out_specs=(P(VEC, ROWS), P(ROWS + VEC, None)),
        check_vma=False,
    )
```

```python
import functools

import jax
import jax.numpy as jnp
from jax import lax
from jax.experimental import pallas as pl
from jax.experimental.pallas import tpu as pltpu
from jax.sharding import Mesh, PartitionSpec as P

BLOCK = 128
STEPS = 4
REACH = 2
HALO = STEPS * REACH
NT = 16
MIB = 1 << 20
ROWS = ("zl", "core")
VEC = ("x", "y", "zh")


def split(value):
    high = value.astype(jnp.bfloat16).astype(jnp.float32)
    return high, value - high


def table_kernel(tiles_ref, table_ref, tiles_here, sems):
    step = NT // sems.shape[0]
    copies = [
        pltpu.make_async_copy(
            tiles_ref.at[at : at + step], tiles_here.at[at : at + step], sems.at[at // step]
        )
        for at in range(0, NT, step)
    ]
    for copy in copies:
        copy.start()
    for tile in range(NT):
        if tile % step == 0:
            copies[tile // step].wait()
        straight = tiles_here[tile]
        flipped = straight.T
        for kind, matrix in enumerate((flipped, straight, (straight + flipped) / 2)):
            high, low = split(matrix)
            entry = tile + NT * kind
            table_ref[entry, :, :BLOCK] = high.astype(jnp.bfloat16)
            table_ref[entry, :, BLOCK:] = low.astype(jnp.bfloat16)


def pack_kernel(
    vectors_ref, offsets_ref, ids_ref, up_ref, down_ref, own_ref, offsets_here, ids_here, sems
):
    edge = up_ref.shape[1] - BLOCK
    rows = vectors_ref.shape[1]
    slots, count = offsets_ref.shape
    copies = [
        pltpu.make_async_copy(source, target, sems.at[at])
        for at, (source, target) in enumerate(
            (
                (offsets_ref, offsets_here),
                (ids_ref, ids_here),
                (vectors_ref.at[:, rows - edge :], up_ref.at[:, :edge]),
                (vectors_ref.at[:, :edge], down_ref.at[:, :edge]),
            )
        )
    ]
    for copy in copies:
        copy.start()
    own_ref[...] = jnp.zeros_like(own_ref)
    copies[0].wait()
    copies[1].wait()
    own_ref[:slots, :count] = offsets_here[...].astype(jnp.float32)
    own_ref[slots : 2 * slots, :count] = ids_here[...].astype(jnp.float32)
    up_ref[:, edge:] = own_ref[...]
    down_ref[:, edge:] = own_ref[...]
    copies[2].wait()
    copies[3].wait()


def filter_kernel(
    vectors_ref, before_ref, after_ref, own_ref, table_ref, bounds_ref,
    filtered_ref, outgoing_ref,
    field_a, field_b, field_c, parts_a, parts_b, plan_vector, plan, sem,
):
    vecs = vectors_ref.shape[0]
    count = vectors_ref.shape[1] // BLOCK
    extent = count + 2 * HALO
    edge = HALO * BLOCK

    lane = lax.broadcasted_iota(jnp.int32, (8, 128), 1)
    row = lax.broadcasted_iota(jnp.int32, (8, 128), 0)
    left = pltpu.roll(before_ref[:, edge:], 128 - (count - HALO), 1)
    own = pltpu.roll(own_ref[...], HALO, 1)
    right = pltpu.roll(after_ref[:, edge:], HALO + count, 1)
    meta = jnp.where(lane < HALO, left, jnp.where(lane < HALO + count, own, right))
    meta = meta.astype(jnp.int32)
    shift = pltpu.roll(meta, 3, 0)
    kind = jnp.where(shift > 0, 0, jnp.where(shift < 0, NT, 2 * NT))
    plan_vector[...] = jnp.where(row < 3, meta + lane, meta + kind)
    copy = pltpu.make_async_copy(plan_vector, plan, sem)
    copy.start()

    def store_parts(target, block, value):
        high, low = split(value)
        target[block] = jnp.concatenate([high, low], axis=0).astype(jnp.bfloat16)

    for block in range(extent):
        if block < HALO:
            value = before_ref[:, block * BLOCK : (block + 1) * BLOCK]
        elif block < HALO + count:
            at = (block - HALO) * BLOCK
            value = vectors_ref[:, at : at + BLOCK]
        else:
            at = (block - HALO - count) * BLOCK
            value = after_ref[:, at : at + BLOCK]
        field_a[block] = value
        store_parts(parts_a, block, value)

    lowest, low_end, high_end = bounds_ref[0], bounds_ref[1], bounds_ref[2]

    def spread(value):
        return jnp.full((vecs, BLOCK), value, jnp.float32)

    half_width = spread((high_end - low_end) * 0.5)
    centre = spread((high_end + low_end) * 0.5)
    sigma_one = half_width / (spread(lowest) - centre)
    sigma_base = 2 / sigma_one
    copy.wait()

    def product(parts, block):
        left_parts, right_parts = [], []
        for slot in range(3):
            left_parts.append(parts[plan[slot, block]])
            right_parts.append(table_ref[plan[3 + slot, block]])
        both = lax.dot_general(
            jnp.concatenate(left_parts, axis=1),
            jnp.concatenate(right_parts, axis=0),
            (((1,), (0,)), ((), ())),
            preferred_element_type=jnp.float32,
        )
        return both[:vecs, :BLOCK] + both[vecs:, :BLOCK] + both[:vecs, BLOCK:]

    fields = [field_a, field_b, field_c, field_a]
    parts = [parts_a, parts_b, parts_a, parts_b]
    sigma = sigma_one
    for step in range(1, STEPS + 1):
        source, source_parts = fields[step - 1], parts[step - 1]
        if step == 1:
            scale, drag = sigma_one / half_width, None
        else:
            following = 1 / (sigma_base - sigma)
            scale, drag = 2 * following / half_width, sigma * following
            sigma = following
        first = REACH * step

        def one_block(block, owner, part):
            value = scale * (product(source_parts, block) - centre * source[block])
            if drag is not None:
                value = value - drag * fields[step - 2][block]
            if step < STEPS:
                fields[step][block] = value
                store_parts(parts[step], block, value)
            else:
                at = block - HALO
                filtered_ref[:, pl.ds(pl.multiple_of(at * BLOCK, BLOCK), BLOCK)] = value
                for copy_at in range(4):
                    outgoing_ref[
                        copy_at * (count // 2) + owner, :, part * BLOCK : (part + 1) * BLOCK
                    ] = value

        group = (extent - 2 * first) // 2

        @pl.loop(0, 2)
        def _(index):
            for inner in range(group):
                one_block(
                    first + index * group + inner, index * (group // 2) + inner // 2, inner % 2
                )


def gram_kernel(scale, stacked_ref, partial_ref, own_high, own_low):
    total = stacked_ref.shape[0]
    group = lax.axis_index("x")
    high, low = split(stacked_ref[...])
    high, low = high.astype(jnp.bfloat16), low.astype(jnp.bfloat16)
    for part in range(8):
        rows = stacked_ref[pl.ds(pl.multiple_of(part * 64 + group * 16, 16), 16), :]
        own, rest = split(rows)
        own_high[part * 16 : (part + 1) * 16, :] = own.astype(jnp.bfloat16)
        own_low[part * 16 : (part + 1) * 16, :] = rest.astype(jnp.bfloat16)
    contract = (((1,), (1,)), ((), ()))

    def multiply(one, other):
        return lax.dot_general(one, other, contract, preferred_element_type=jnp.float32)

    a_high, a_low = own_high[...], own_low[...]
    partial = multiply(a_high, high) + multiply(a_high, low) + multiply(a_low, high)
    partial = partial * scale
    count = partial.shape[0]
    pieces = total // BLOCK
    for piece in range(pieces):
        partial_ref[pl.ds(piece, count, stride=pieces), :] = partial[
            :, piece * BLOCK : (piece + 1) * BLOCK
        ]


def on_device(vectors, tile_table, offsets, tile_ids, bounds):
    vecs, local_rows = vectors.shape
    count = local_rows // BLOCK
    extent = count + 2 * HALO
    edge = HALO * BLOCK
    size = lax.axis_size(ROWS)
    up = [(i, i + 1) for i in range(size - 1)]
    down = [(j, i) for i, j in up]
    vmem = pl.BlockSpec(memory_space=pltpu.VMEM)
    smem = pl.BlockSpec(memory_space=pltpu.SMEM)
    hbm = pl.BlockSpec(memory_space=pltpu.HBM)
    packed = jax.ShapeDtypeStruct((vecs, edge + BLOCK), jnp.float32)
    slots = pltpu.VMEM((3, count), jnp.int32)
    to_upper, to_lower, meta = pl.pallas_call(
        pack_kernel,
        out_shape=(packed, packed, jax.ShapeDtypeStruct((8, BLOCK), jnp.float32)),
        in_specs=[hbm, hbm, hbm],
        out_specs=(vmem, vmem, vmem),
        scratch_shapes=[slots, slots, pltpu.SemaphoreType.DMA((4,))],
        compiler_params=pltpu.CompilerParams(vmem_limit_bytes=4 * MIB),
        name="pack",
    )(*(
        pltpu.with_memory_space_constraint(array, pltpu.HBM)
        for array in (vectors, offsets.T, tile_ids.T)
    ))
    before = lax.ppermute(to_upper, ROWS, up)
    after = lax.ppermute(to_lower, ROWS, down)

    table = pl.pallas_call(
        table_kernel,
        out_shape=jax.ShapeDtypeStruct((3 * NT, BLOCK, 2 * BLOCK), jnp.bfloat16),
        in_specs=[hbm],
        out_specs=vmem,
        scratch_shapes=[
            pltpu.VMEM(tile_table.shape, jnp.float32),
            pltpu.SemaphoreType.DMA((4,)),
        ],
        compiler_params=pltpu.CompilerParams(vmem_limit_bytes=16 * MIB),
        name="table",
    )(pltpu.with_memory_space_constraint(tile_table, pltpu.HBM))

    field = pltpu.VMEM((extent, vecs, BLOCK), jnp.float32)
    parts = pltpu.VMEM((extent, 2 * vecs, BLOCK), jnp.bfloat16)
    filtered, outgoing = pl.pallas_call(
        filter_kernel,
        out_shape=(
            jax.ShapeDtypeStruct((vecs, local_rows), jnp.float32),
            jax.ShapeDtypeStruct((64, vecs, 2 * BLOCK), jnp.float32),
        ),
        in_specs=[vmem, vmem, vmem, vmem, vmem, smem],
        out_specs=(vmem, vmem),
        scratch_shapes=[
            field, field, field, parts, parts,
            pltpu.VMEM((8, BLOCK), jnp.int32),
            pltpu.SMEM((8, BLOCK), jnp.int32),
            pltpu.SemaphoreType.DMA(()),
        ],
        compiler_params=pltpu.CompilerParams(vmem_limit_bytes=16 * MIB),
        name="filter",
    )(vectors, before, after, meta, table, bounds)

    stacked = lax.all_to_all(outgoing, VEC, split_axis=0, concat_axis=0, tiled=True)
    total = 64 * vecs
    stacked = stacked.reshape(total, 2 * BLOCK)
    owned = total // 4
    partial = pl.pallas_call(
        functools.partial(gram_kernel, 1.0 / (local_rows * size)),
        out_shape=jax.ShapeDtypeStruct((owned * (total // BLOCK), BLOCK), jnp.float32),
        in_specs=[vmem],
        out_specs=vmem,
        scratch_shapes=[pltpu.VMEM((owned, 2 * BLOCK), jnp.bfloat16)] * 2,
        compiler_params=pltpu.CompilerParams(vmem_limit_bytes=16 * MIB),
        name="gram",
    )(stacked)
    received = lax.all_to_all(
        partial.reshape(owned, 1, total),
        ROWS + ("y", "zh"),
        split_axis=0,
        concat_axis=0,
        tiled=True,
    )
    gram_matrix = jnp.sum(received, axis=0)
    return filtered, gram_matrix


def solution(mesh):
    fine = Mesh(mesh.devices.reshape(4, 2, 4, 8, 2), ROWS + VEC)
    placed = (P(VEC, ROWS), P(), P(ROWS, None), P(ROWS, None), P())
    return jax.shard_map(
        on_device,
        mesh=fine,
        in_specs=placed,
        out_specs=(P(VEC, ROWS), P(ROWS + VEC, None)),
        check_vma=False,
    )
```

```python
import functools

import jax
import jax.numpy as jnp
from jax import lax
from jax.experimental import pallas as pl
from jax.experimental.pallas import tpu as pltpu
from jax.sharding import Mesh, PartitionSpec as P

BLOCK = 128
STEPS = 4
REACH = 2
HALO = STEPS * REACH
NT = 16
MIB = 1 << 20
ROWS = ("zl", "core")
VEC = ("x", "y", "zh")
FIRST_TURN = 0b101001
SECOND_TURN = 0b1101000


def split(value):
    high = value.astype(jnp.bfloat16).astype(jnp.float32)
    return high, value - high


def table_kernel(tiles_ref, table_ref, tiles_here, sems):
    step = NT // sems.shape[0]
    copies = [
        pltpu.make_async_copy(
            tiles_ref.at[at : at + step], tiles_here.at[at : at + step], sems.at[at // step]
        )
        for at in range(0, NT, step)
    ]
    for copy in copies:
        copy.start()
    for tile in range(NT):
        if tile % step == 0:
            copies[tile // step].wait()
        straight = tiles_here[tile]
        flipped = straight.T
        for kind, matrix in enumerate((flipped, straight, (straight + flipped) / 2)):
            high, low = split(matrix)
            entry = tile + NT * kind
            table_ref[entry, :, :BLOCK] = high.astype(jnp.bfloat16)
            table_ref[entry, :, BLOCK:] = low.astype(jnp.bfloat16)


def pack_kernel(
    vectors_ref, offsets_ref, ids_ref, up_ref, down_ref, own_ref, offsets_here, ids_here, sems
):
    edge = up_ref.shape[1] - BLOCK
    rows = vectors_ref.shape[1]
    slots, count = offsets_ref.shape
    copies = [
        pltpu.make_async_copy(source, target, sems.at[at])
        for at, (source, target) in enumerate(
            (
                (offsets_ref, offsets_here),
                (ids_ref, ids_here),
                (vectors_ref.at[:, rows - edge :], up_ref.at[:, :edge]),
                (vectors_ref.at[:, :edge], down_ref.at[:, :edge]),
            )
        )
    ]
    for copy in copies:
        copy.start()
    own_ref[...] = jnp.zeros_like(own_ref)
    copies[0].wait()
    copies[1].wait()
    own_ref[:slots, :count] = offsets_here[...].astype(jnp.float32)
    own_ref[slots : 2 * slots, :count] = ids_here[...].astype(jnp.float32)
    up_ref[:, edge:] = own_ref[...]
    down_ref[:, edge:] = own_ref[...]
    copies[2].wait()
    copies[3].wait()


def filter_kernel(
    vectors_ref, before_ref, after_ref, own_ref, table_ref, bounds_ref,
    filtered_ref, outgoing_ref,
    field_a, field_b, field_c, parts_a, parts_b, plan_vector, plan, sem,
):
    vecs = vectors_ref.shape[0]
    count = vectors_ref.shape[1] // BLOCK
    extent = count + 2 * HALO
    edge = HALO * BLOCK

    lane = lax.broadcasted_iota(jnp.int32, (8, 128), 1)
    row = lax.broadcasted_iota(jnp.int32, (8, 128), 0)
    left = pltpu.roll(before_ref[:, edge:], 128 - (count - HALO), 1)
    own = pltpu.roll(own_ref[...], HALO, 1)
    right = pltpu.roll(after_ref[:, edge:], HALO + count, 1)
    meta = jnp.where(lane < HALO, left, jnp.where(lane < HALO + count, own, right))
    meta = meta.astype(jnp.int32)
    shift = pltpu.roll(meta, 3, 0)
    kind = jnp.where(shift > 0, 0, jnp.where(shift < 0, NT, 2 * NT))
    plan_vector[...] = jnp.where(row < 3, meta + lane, meta + kind)
    copy = pltpu.make_async_copy(plan_vector, plan, sem)
    copy.start()

    def store_parts(target, block, value):
        high, low = split(value)
        target[block] = jnp.concatenate([high, low], axis=0).astype(jnp.bfloat16)

    for block in range(extent):
        if block < HALO:
            value = before_ref[:, block * BLOCK : (block + 1) * BLOCK]
        elif block < HALO + count:
            at = (block - HALO) * BLOCK
            value = vectors_ref[:, at : at + BLOCK]
        else:
            at = (block - HALO - count) * BLOCK
            value = after_ref[:, at : at + BLOCK]
        field_a[block] = value
        store_parts(parts_a, block, value)

    lowest, low_end, high_end = bounds_ref[0], bounds_ref[1], bounds_ref[2]

    def spread(value):
        return jnp.full((vecs, BLOCK), value, jnp.float32)

    half_width = spread((high_end - low_end) * 0.5)
    centre = spread((high_end + low_end) * 0.5)
    sigma_one = half_width / (spread(lowest) - centre)
    sigma_base = 2 / sigma_one
    copy.wait()

    def product(parts, block):
        left_parts, right_parts = [], []
        for slot in range(3):
            left_parts.append(parts[plan[slot, block]])
            right_parts.append(table_ref[plan[3 + slot, block]])
        both = lax.dot_general(
            jnp.concatenate(left_parts, axis=1),
            jnp.concatenate(right_parts, axis=0),
            (((1,), (0,)), ((), ())),
            preferred_element_type=jnp.float32,
        )
        return both[:vecs, :BLOCK] + both[vecs:, :BLOCK] + both[:vecs, BLOCK:]

    fields = [field_a, field_b, field_c, field_a]
    parts = [parts_a, parts_b, parts_a, parts_b]
    sigma = sigma_one
    for step in range(1, STEPS + 1):
        source, source_parts = fields[step - 1], parts[step - 1]
        if step == 1:
            scale, drag = sigma_one / half_width, None
        else:
            following = 1 / (sigma_base - sigma)
            scale, drag = 2 * following / half_width, sigma * following
            sigma = following
        first = REACH * step

        def one_block(block, owner, part):
            value = scale * (product(source_parts, block) - centre * source[block])
            if drag is not None:
                value = value - drag * fields[step - 2][block]
            if step < STEPS:
                fields[step][block] = value
                store_parts(parts[step], block, value)
            else:
                at = block - HALO
                filtered_ref[:, pl.ds(pl.multiple_of(at * BLOCK, BLOCK), BLOCK)] = value
                for copy_at in range(4):
                    outgoing_ref[
                        copy_at * (count // 2) + owner, :, part * BLOCK : (part + 1) * BLOCK
                    ] = value

        group = (extent - 2 * first) // 2

        @pl.loop(0, 2)
        def _(index):
            for inner in range(group):
                turn = FIRST_TURN % (count // 2)
                half = group // 2
                owner = (index ^ (turn // half)) * half + ((inner // 2) ^ (turn % half))
                one_block(first + index * group + inner, owner, inner % 2)


def gram_kernel(scale, stacked_ref, partial_ref, all_high, all_low, own_high, own_low):
    total = stacked_ref.shape[0]
    group = lax.axis_index("x")

    def arrived(one, other):
        tiles = [
            stacked_ref[pl.ds(pl.multiple_of((at ^ FIRST_TURN) * 8, 8), 8), :] for at in (one, other)
        ]
        high, low = split(jnp.concatenate(tiles, axis=0))
        return high.astype(jnp.bfloat16), low.astype(jnp.bfloat16)

    for pair in range(total // 16):
        rows = slice(pair * 16, (pair + 1) * 16)
        all_high[rows, :], all_low[rows, :] = arrived(2 * pair, 2 * pair + 1)
    for slot in range(8):
        owner = (slot ^ (SECOND_TURN // 16)) * 8 + group * 2
        swap = (SECOND_TURN % 16) // 8
        rows = slice(slot * 16, (slot + 1) * 16)
        own_high[rows, :], own_low[rows, :] = arrived(owner + swap, owner + 1 - swap)
    contract = (((1,), (1,)), ((), ()))

    def multiply(one, other):
        return lax.dot_general(one, other, contract, preferred_element_type=jnp.float32)

    high, low = all_high[...], all_low[...]
    a_high, a_low = own_high[...], own_low[...]
    partial = multiply(a_high, high) + multiply(a_high, low) + multiply(a_low, high)
    partial = partial * scale
    count = partial.shape[0]
    pieces = total // BLOCK
    for piece in range(pieces):
        partial_ref[pl.ds(piece, count, stride=pieces), :] = partial[
            :, piece * BLOCK : (piece + 1) * BLOCK
        ]


def on_device(vectors, tile_table, offsets, tile_ids, bounds):
    vecs, local_rows = vectors.shape
    count = local_rows // BLOCK
    extent = count + 2 * HALO
    edge = HALO * BLOCK
    size = lax.axis_size(ROWS)
    up = [(i, i + 1) for i in range(size - 1)]
    down = [(j, i) for i, j in up]
    vmem = pl.BlockSpec(memory_space=pltpu.VMEM)
    smem = pl.BlockSpec(memory_space=pltpu.SMEM)
    hbm = pl.BlockSpec(memory_space=pltpu.HBM)
    packed = jax.ShapeDtypeStruct((vecs, edge + BLOCK), jnp.float32)
    slots = pltpu.VMEM((3, count), jnp.int32)
    to_upper, to_lower, meta = pl.pallas_call(
        pack_kernel,
        out_shape=(packed, packed, jax.ShapeDtypeStruct((8, BLOCK), jnp.float32)),
        in_specs=[hbm, hbm, hbm],
        out_specs=(vmem, vmem, vmem),
        scratch_shapes=[slots, slots, pltpu.SemaphoreType.DMA((4,))],
        compiler_params=pltpu.CompilerParams(vmem_limit_bytes=4 * MIB),
        name="pack",
    )(*(
        pltpu.with_memory_space_constraint(array, pltpu.HBM)
        for array in (vectors, offsets.T, tile_ids.T)
    ))
    before = lax.ppermute(to_upper, ROWS, up)
    after = lax.ppermute(to_lower, ROWS, down)

    table = pl.pallas_call(
        table_kernel,
        out_shape=jax.ShapeDtypeStruct((3 * NT, BLOCK, 2 * BLOCK), jnp.bfloat16),
        in_specs=[hbm],
        out_specs=vmem,
        scratch_shapes=[
            pltpu.VMEM(tile_table.shape, jnp.float32),
            pltpu.SemaphoreType.DMA((4,)),
        ],
        compiler_params=pltpu.CompilerParams(vmem_limit_bytes=16 * MIB),
        name="table",
    )(pltpu.with_memory_space_constraint(tile_table, pltpu.HBM))

    field = pltpu.VMEM((extent, vecs, BLOCK), jnp.float32)
    parts = pltpu.VMEM((extent, 2 * vecs, BLOCK), jnp.bfloat16)
    filtered, outgoing = pl.pallas_call(
        filter_kernel,
        out_shape=(
            jax.ShapeDtypeStruct((vecs, local_rows), jnp.float32),
            jax.ShapeDtypeStruct((64, vecs, 2 * BLOCK), jnp.float32),
        ),
        in_specs=[vmem, vmem, vmem, vmem, vmem, smem],
        out_specs=(vmem, vmem),
        scratch_shapes=[
            field, field, field, parts, parts,
            pltpu.VMEM((8, BLOCK), jnp.int32),
            pltpu.SMEM((8, BLOCK), jnp.int32),
            pltpu.SemaphoreType.DMA(()),
        ],
        compiler_params=pltpu.CompilerParams(vmem_limit_bytes=16 * MIB),
        name="filter",
    )(vectors, before, after, meta, table, bounds)

    stacked = lax.all_to_all(
        outgoing,
        VEC,
        split_axis=0,
        concat_axis=0,
        tiled=True,
        axis_index_groups=[[at ^ FIRST_TURN for at in range(64)]],
    )
    total = 64 * vecs
    stacked = stacked.reshape(total, 2 * BLOCK)
    owned = total // 4
    partial = pl.pallas_call(
        functools.partial(gram_kernel, 1.0 / (local_rows * size)),
        out_shape=jax.ShapeDtypeStruct((owned * (total // BLOCK), BLOCK), jnp.float32),
        in_specs=[vmem],
        out_specs=vmem,
        scratch_shapes=[pltpu.VMEM((total, 2 * BLOCK), jnp.bfloat16)] * 2
        + [pltpu.VMEM((owned, 2 * BLOCK), jnp.bfloat16)] * 2,
        compiler_params=pltpu.CompilerParams(vmem_limit_bytes=16 * MIB),
        name="gram",
    )(stacked)
    received = lax.all_to_all(
        partial.reshape(owned, 1, total),
        ROWS + ("y", "zh"),
        split_axis=0,
        concat_axis=0,
        tiled=True,
        axis_index_groups=[[at ^ SECOND_TURN for at in range(owned)]],
    )
    gram_matrix = jnp.sum(received, axis=0)
    return filtered, gram_matrix


def solution(mesh):
    fine = Mesh(mesh.devices.reshape(4, 2, 4, 8, 2), ROWS + VEC)
    placed = (P(VEC, ROWS), P(), P(ROWS, None), P(ROWS, None), P())
    return jax.shard_map(
        on_device,
        mesh=fine,
        in_specs=placed,
        out_specs=(P(VEC, ROWS), P(ROWS + VEC, None)),
        check_vma=False,
    )
```

```python
import functools

import jax
import jax.numpy as jnp
from jax import lax
from jax.experimental import pallas as pl
from jax.experimental.pallas import tpu as pltpu
from jax.sharding import Mesh, PartitionSpec as P

BLOCK = 128
STEPS = 4
REACH = 2
HALO = STEPS * REACH
NT = 16
MIB = 1 << 20
ROWS = ("zl", "core")
VEC = ("x", "yq", "yb", "zh")
OWNERS = ROWS + ("x", "yb", "zh")
FIRST_TURN = 0b101001
SECOND_TURN = 0b1101000


def split(value):
    high = value.astype(jnp.bfloat16).astype(jnp.float32)
    return high, value - high


def table_kernel(tiles_ref, table_ref, tiles_here, sems):
    step = NT // sems.shape[0]
    copies = [
        pltpu.make_async_copy(
            tiles_ref.at[at : at + step], tiles_here.at[at : at + step], sems.at[at // step]
        )
        for at in range(0, NT, step)
    ]
    for copy in copies:
        copy.start()
    for tile in range(NT):
        if tile % step == 0:
            copies[tile // step].wait()
        straight = tiles_here[tile]
        flipped = straight.T
        for kind, matrix in enumerate((flipped, straight, (straight + flipped) / 2)):
            high, low = split(matrix)
            entry = tile + NT * kind
            table_ref[entry, :, :BLOCK] = high.astype(jnp.bfloat16)
            table_ref[entry, :, BLOCK:] = low.astype(jnp.bfloat16)


def pack_kernel(
    vectors_ref, offsets_ref, ids_ref, up_ref, down_ref, own_ref, offsets_here, ids_here, sems
):
    edge = up_ref.shape[1] - BLOCK
    rows = vectors_ref.shape[1]
    slots, count = offsets_ref.shape
    copies = [
        pltpu.make_async_copy(source, target, sems.at[at])
        for at, (source, target) in enumerate(
            (
                (offsets_ref, offsets_here),
                (ids_ref, ids_here),
                (vectors_ref.at[:, rows - edge :], up_ref.at[:, :edge]),
                (vectors_ref.at[:, :edge], down_ref.at[:, :edge]),
            )
        )
    ]
    for copy in copies:
        copy.start()
    own_ref[...] = jnp.zeros_like(own_ref)
    copies[0].wait()
    copies[1].wait()
    own_ref[:slots, :count] = offsets_here[...].astype(jnp.float32)
    own_ref[slots : 2 * slots, :count] = ids_here[...].astype(jnp.float32)
    up_ref[:, edge:] = own_ref[...]
    down_ref[:, edge:] = own_ref[...]
    copies[2].wait()
    copies[3].wait()


def filter_kernel(
    vectors_ref, before_ref, after_ref, own_ref, table_ref, bounds_ref,
    filtered_ref, outgoing_ref,
    field_a, field_b, field_c, parts_a, parts_b, plan_vector, plan, sem,
):
    vecs = vectors_ref.shape[0]
    count = vectors_ref.shape[1] // BLOCK
    extent = count + 2 * HALO
    edge = HALO * BLOCK

    lane = lax.broadcasted_iota(jnp.int32, (8, 128), 1)
    row = lax.broadcasted_iota(jnp.int32, (8, 128), 0)
    left = pltpu.roll(before_ref[:, edge:], 128 - (count - HALO), 1)
    own = pltpu.roll(own_ref[...], HALO, 1)
    right = pltpu.roll(after_ref[:, edge:], HALO + count, 1)
    meta = jnp.where(lane < HALO, left, jnp.where(lane < HALO + count, own, right))
    meta = meta.astype(jnp.int32)
    shift = pltpu.roll(meta, 3, 0)
    kind = jnp.where(shift > 0, 0, jnp.where(shift < 0, NT, 2 * NT))
    plan_vector[...] = jnp.where(row < 3, meta + lane, meta + kind)
    copy = pltpu.make_async_copy(plan_vector, plan, sem)
    copy.start()

    def store_parts(target, block, value):
        high, low = split(value)
        target[block] = jnp.concatenate([high, low], axis=0).astype(jnp.bfloat16)

    for block in range(extent):
        if block < HALO:
            value = before_ref[:, block * BLOCK : (block + 1) * BLOCK]
        elif block < HALO + count:
            at = (block - HALO) * BLOCK
            value = vectors_ref[:, at : at + BLOCK]
        else:
            at = (block - HALO - count) * BLOCK
            value = after_ref[:, at : at + BLOCK]
        field_a[block] = value
        store_parts(parts_a, block, value)

    lowest, low_end, high_end = bounds_ref[0], bounds_ref[1], bounds_ref[2]

    def spread(value):
        return jnp.full((vecs, BLOCK), value, jnp.float32)

    half_width = spread((high_end - low_end) * 0.5)
    centre = spread((high_end + low_end) * 0.5)
    sigma_one = half_width / (spread(lowest) - centre)
    sigma_base = 2 / sigma_one
    copy.wait()

    def product(parts, block):
        left_parts, right_parts = [], []
        for slot in range(3):
            left_parts.append(parts[plan[slot, block]])
            right_parts.append(table_ref[plan[3 + slot, block]])
        both = lax.dot_general(
            jnp.concatenate(left_parts, axis=1),
            jnp.concatenate(right_parts, axis=0),
            (((1,), (0,)), ((), ())),
            preferred_element_type=jnp.float32,
        )
        return both[:vecs, :BLOCK] + both[vecs:, :BLOCK] + both[:vecs, BLOCK:]

    fields = [field_a, field_b, field_c, field_a]
    parts = [parts_a, parts_b, parts_a, parts_b]
    sigma = sigma_one
    for step in range(1, STEPS + 1):
        source, source_parts = fields[step - 1], parts[step - 1]
        if step == 1:
            scale, drag = sigma_one / half_width, None
        else:
            following = 1 / (sigma_base - sigma)
            scale, drag = 2 * following / half_width, sigma * following
            sigma = following
        first = REACH * step

        def one_block(block, owner, part):
            value = scale * (product(source_parts, block) - centre * source[block])
            if drag is not None:
                value = value - drag * fields[step - 2][block]
            if step < STEPS:
                fields[step][block] = value
                store_parts(parts[step], block, value)
            else:
                at = block - HALO
                filtered_ref[:, pl.ds(pl.multiple_of(at * BLOCK, BLOCK), BLOCK)] = value
                upper, lower = owner
                for quarter in range(4):
                    inner = (lower // 4 * 16 + quarter * 4 + lower % 4) ^ (FIRST_TURN % 32)
                    outgoing_ref[
                        (upper ^ (FIRST_TURN // 32)) * 32 + inner,
                        :,
                        part * BLOCK : (part + 1) * BLOCK,
                    ] = value

        group = (extent - 2 * first) // 2

        @pl.loop(0, 2)
        def _(index):
            for inner in range(group):
                one_block(first + index * group + inner, (index, inner // 2), inner % 2)


def gram_kernel(scale, stacked_ref, partial_ref, all_high, all_low, own_high, own_low):
    total = stacked_ref.shape[0]
    quarter = lax.axis_index("yq")

    def arrived(at):
        return stacked_ref[pl.ds(pl.multiple_of((at ^ FIRST_TURN) * 8, 8), 8), :]

    def store(high_ref, low_ref, at, tiles):
        high, low = split(jnp.concatenate(tiles, axis=0))
        high_ref[at * 16 : (at + 1) * 16, :] = high.astype(jnp.bfloat16)
        low_ref[at * 16 : (at + 1) * 16, :] = low.astype(jnp.bfloat16)

    for pair in range(total // 16):
        store(all_high, all_low, pair, [arrived(2 * pair), arrived(2 * pair + 1)])

    upper_rows = lax.broadcasted_iota(jnp.int32, (8, stacked_ref.shape[1]), 0) < 4
    odd = quarter % 2 == 1

    def owned_tile(at):
        tiles = [arrived((slot ^ (SECOND_TURN // 4)) * 2 + quarter // 2) for slot in (at, at + 1)]
        turned = [pltpu.roll(tile, 4, 0) for tile in tiles]
        first = jnp.where(odd, turned[0], tiles[0])
        second = jnp.where(odd, tiles[1], turned[1])
        return jnp.where(upper_rows, first, second)

    for quad in range(8):
        store(own_high, own_low, quad, [owned_tile(4 * quad), owned_tile(4 * quad + 2)])
    contract = (((1,), (1,)), ((), ()))

    def multiply(one, other):
        return lax.dot_general(one, other, contract, preferred_element_type=jnp.float32)

    high, low = all_high[...], all_low[...]
    a_high, a_low = own_high[...], own_low[...]
    partial = multiply(a_high, high) + multiply(a_high, low) + multiply(a_low, high)
    partial = partial * scale
    count = partial.shape[0]
    pieces = total // BLOCK
    for piece in range(pieces):
        partial_ref[pl.ds(piece, count, stride=pieces), :] = partial[
            :, piece * BLOCK : (piece + 1) * BLOCK
        ]


def on_device(vectors, tile_table, offsets, tile_ids, bounds):
    vecs, local_rows = vectors.shape
    count = local_rows // BLOCK
    extent = count + 2 * HALO
    edge = HALO * BLOCK
    size = lax.axis_size(ROWS)
    up = [(i, i + 1) for i in range(size - 1)]
    down = [(j, i) for i, j in up]
    vmem = pl.BlockSpec(memory_space=pltpu.VMEM)
    smem = pl.BlockSpec(memory_space=pltpu.SMEM)
    hbm = pl.BlockSpec(memory_space=pltpu.HBM)
    packed = jax.ShapeDtypeStruct((vecs, edge + BLOCK), jnp.float32)
    slots = pltpu.VMEM((3, count), jnp.int32)
    to_upper, to_lower, meta = pl.pallas_call(
        pack_kernel,
        out_shape=(packed, packed, jax.ShapeDtypeStruct((8, BLOCK), jnp.float32)),
        in_specs=[hbm, hbm, hbm],
        out_specs=(vmem, vmem, vmem),
        scratch_shapes=[slots, slots, pltpu.SemaphoreType.DMA((4,))],
        compiler_params=pltpu.CompilerParams(vmem_limit_bytes=4 * MIB),
        name="pack",
    )(*(
        pltpu.with_memory_space_constraint(array, pltpu.HBM)
        for array in (vectors, offsets.T, tile_ids.T)
    ))
    before = lax.ppermute(to_upper, ROWS, up)
    after = lax.ppermute(to_lower, ROWS, down)

    table = pl.pallas_call(
        table_kernel,
        out_shape=jax.ShapeDtypeStruct((3 * NT, BLOCK, 2 * BLOCK), jnp.bfloat16),
        in_specs=[hbm],
        out_specs=vmem,
        scratch_shapes=[
            pltpu.VMEM(tile_table.shape, jnp.float32),
            pltpu.SemaphoreType.DMA((4,)),
        ],
        compiler_params=pltpu.CompilerParams(vmem_limit_bytes=16 * MIB),
        name="table",
    )(pltpu.with_memory_space_constraint(tile_table, pltpu.HBM))

    field = pltpu.VMEM((extent, vecs, BLOCK), jnp.float32)
    parts = pltpu.VMEM((extent, 2 * vecs, BLOCK), jnp.bfloat16)
    filtered, outgoing = pl.pallas_call(
        filter_kernel,
        out_shape=(
            jax.ShapeDtypeStruct((vecs, local_rows), jnp.float32),
            jax.ShapeDtypeStruct((64, vecs, 2 * BLOCK), jnp.float32),
        ),
        in_specs=[vmem, vmem, vmem, vmem, vmem, smem],
        out_specs=(vmem, vmem),
        scratch_shapes=[
            field, field, field, parts, parts,
            pltpu.VMEM((8, BLOCK), jnp.int32),
            pltpu.SMEM((8, BLOCK), jnp.int32),
            pltpu.SemaphoreType.DMA(()),
        ],
        compiler_params=pltpu.CompilerParams(vmem_limit_bytes=16 * MIB),
        name="filter",
    )(vectors, before, after, meta, table, bounds)

    stacked = lax.all_to_all(
        outgoing,
        VEC,
        split_axis=0,
        concat_axis=0,
        tiled=True,
        axis_index_groups=[[at ^ FIRST_TURN for at in range(64)]],
    )
    total = 64 * vecs
    stacked = stacked.reshape(total, 2 * BLOCK)
    owned = total // 4
    partial = pl.pallas_call(
        functools.partial(gram_kernel, 1.0 / (local_rows * size)),
        out_shape=jax.ShapeDtypeStruct((owned * (total // BLOCK), BLOCK), jnp.float32),
        in_specs=[vmem],
        out_specs=vmem,
        scratch_shapes=[pltpu.VMEM((total, 2 * BLOCK), jnp.bfloat16)] * 2
        + [pltpu.VMEM((owned, 2 * BLOCK), jnp.bfloat16)] * 2,
        compiler_params=pltpu.CompilerParams(vmem_limit_bytes=16 * MIB),
        name="gram",
    )(stacked)
    received = lax.all_to_all(
        partial.reshape(owned, 1, total),
        OWNERS,
        split_axis=0,
        concat_axis=0,
        tiled=True,
        axis_index_groups=[[at ^ SECOND_TURN for at in range(owned)]],
    )
    gram_matrix = jnp.sum(received, axis=0)
    return filtered, gram_matrix


def solution(mesh):
    fine = Mesh(mesh.devices.reshape(4, 2, 4, 4, 2, 2), ROWS + VEC)
    placed = (P(VEC, ROWS), P(), P(ROWS, None), P(ROWS, None), P())
    return jax.shard_map(
        on_device,
        mesh=fine,
        in_specs=placed,
        out_specs=(P(VEC, ROWS), P(ROWS + VEC, None)),
        check_vma=False,
    )
```

```python
import functools

import jax
import jax.numpy as jnp
from jax import lax
from jax.experimental import pallas as pl
from jax.experimental.pallas import tpu as pltpu
from jax.sharding import Mesh, PartitionSpec as P

BLOCK = 128
STEPS = 4
REACH = 2
HALO = STEPS * REACH
NT = 16
MIB = 1 << 20
ROWS = ("zl", "core")
VEC = ("x", "yq", "yb", "zh")
OWNERS = ROWS + ("x", "yb", "zh")
FIRST_TURN = 0b101000
SECOND_TURN = 0b1101000


def split(value):
    high = value.astype(jnp.bfloat16).astype(jnp.float32)
    return high, value - high


def table_kernel(tiles_ref, table_ref):
    for tile in range(NT):
        straight = tiles_ref[tile]
        flipped = straight.T
        for kind, matrix in enumerate((flipped, straight, (straight + flipped) / 2)):
            high, low = split(matrix)
            entry = tile + NT * kind
            table_ref[entry, :, :BLOCK] = high.astype(jnp.bfloat16)
            table_ref[entry, :, BLOCK:] = low.astype(jnp.bfloat16)


def pack_kernel(
    vectors_ref, offsets_ref, ids_ref, tiles_ref,
    up_ref, down_ref, own_ref, tiles_here, offsets_here, ids_here, sems,
):
    edge = up_ref.shape[1] - BLOCK
    rows = vectors_ref.shape[1]
    slots, count = offsets_ref.shape
    copies = [
        pltpu.make_async_copy(source, target, sems.at[at])
        for at, (source, target) in enumerate(
            (
                (offsets_ref, offsets_here),
                (ids_ref, ids_here),
                (vectors_ref.at[:, rows - edge :], up_ref.at[:, :edge]),
                (vectors_ref.at[:, :edge], down_ref.at[:, :edge]),
                (tiles_ref, tiles_here),
            )
        )
    ]
    for copy in copies:
        copy.start()
    own_ref[...] = jnp.zeros_like(own_ref)
    copies[0].wait()
    copies[1].wait()
    own_ref[:slots, :count] = offsets_here[...].astype(jnp.float32)
    own_ref[slots : 2 * slots, :count] = ids_here[...].astype(jnp.float32)
    up_ref[:, edge:] = own_ref[...]
    down_ref[:, edge:] = own_ref[...]
    for copy in copies[2:]:
        copy.wait()


def filter_kernel(
    vectors_ref, before_ref, after_ref, own_ref, table_ref, bounds_ref,
    filtered_ref, outgoing_ref,
    field_a, field_b, field_c, parts_a, parts_b, plan_vector, plan, sem,
):
    vecs = vectors_ref.shape[0]
    count = vectors_ref.shape[1] // BLOCK
    extent = count + 2 * HALO
    edge = HALO * BLOCK

    lane = lax.broadcasted_iota(jnp.int32, (8, 128), 1)
    row = lax.broadcasted_iota(jnp.int32, (8, 128), 0)
    left = pltpu.roll(before_ref[:, edge:], 128 - (count - HALO), 1)
    own = pltpu.roll(own_ref[...], HALO, 1)
    right = pltpu.roll(after_ref[:, edge:], HALO + count, 1)
    meta = jnp.where(lane < HALO, left, jnp.where(lane < HALO + count, own, right))
    meta = meta.astype(jnp.int32)
    shift = pltpu.roll(meta, 3, 0)
    kind = jnp.where(shift > 0, 0, jnp.where(shift < 0, NT, 2 * NT))
    plan_vector[...] = jnp.where(row < 3, meta + lane, meta + kind)
    copy = pltpu.make_async_copy(plan_vector, plan, sem)
    copy.start()

    def store_parts(target, block, value):
        high, low = split(value)
        target[block] = jnp.concatenate([high, low], axis=0).astype(jnp.bfloat16)

    for block in range(extent):
        if block < HALO:
            value = before_ref[:, block * BLOCK : (block + 1) * BLOCK]
        elif block < HALO + count:
            at = (block - HALO) * BLOCK
            value = vectors_ref[:, at : at + BLOCK]
        else:
            at = (block - HALO - count) * BLOCK
            value = after_ref[:, at : at + BLOCK]
        field_a[block] = value
        store_parts(parts_a, block, value)

    lowest, low_end, high_end = bounds_ref[0], bounds_ref[1], bounds_ref[2]

    def spread(value):
        return jnp.full((vecs, BLOCK), value, jnp.float32)

    half_width = spread((high_end - low_end) * 0.5)
    centre = spread((high_end + low_end) * 0.5)
    sigma_one = half_width / (spread(lowest) - centre)
    sigma_base = 2 / sigma_one
    copy.wait()

    def product(parts, block):
        left_parts, right_parts = [], []
        for slot in range(3):
            left_parts.append(parts[plan[slot, block]])
            right_parts.append(table_ref[plan[3 + slot, block]])
        both = lax.dot_general(
            jnp.concatenate(left_parts, axis=1),
            jnp.concatenate(right_parts, axis=0),
            (((1,), (0,)), ((), ())),
            preferred_element_type=jnp.float32,
        )
        return both[:vecs, :BLOCK] + both[vecs:, :BLOCK] + both[:vecs, BLOCK:]

    fields = [field_a, field_b, field_c, field_a]
    parts = [parts_a, parts_b, parts_a, parts_b]
    sigma = sigma_one
    for step in range(1, STEPS + 1):
        source, source_parts = fields[step - 1], parts[step - 1]
        if step == 1:
            scale, drag = sigma_one / half_width, None
        else:
            following = 1 / (sigma_base - sigma)
            scale, drag = 2 * following / half_width, sigma * following
            sigma = following
        first = REACH * step

        def one_block(block, owner, part):
            value = scale * (product(source_parts, block) - centre * source[block])
            if drag is not None:
                value = value - drag * fields[step - 2][block]
            if step < STEPS:
                fields[step][block] = value
                store_parts(parts[step], block, value)
            else:
                at = block - HALO
                filtered_ref[:, pl.ds(pl.multiple_of(at * BLOCK, BLOCK), BLOCK)] = value
                upper, lower = owner
                for quarter in range(4):
                    inner = (lower // 4 * 16 + quarter * 4 + lower % 4) ^ (FIRST_TURN % 32)
                    outgoing_ref[
                        (upper ^ (FIRST_TURN // 32)) * 32 + inner,
                        :,
                        part * BLOCK : (part + 1) * BLOCK,
                    ] = value

        group = (extent - 2 * first) // 2

        @pl.loop(0, 2)
        def _(index):
            for inner in range(group):
                one_block(first + index * group + inner, (index, inner // 2), inner % 2)


def gram_kernel(scale, stacked_ref, partial_ref, all_high, all_low, own_high, own_low):
    total = stacked_ref.shape[0]
    quarter = lax.axis_index("yq")

    def arrived(at):
        return stacked_ref[pl.ds(pl.multiple_of((at ^ FIRST_TURN) * 8, 8), 8), :]

    def store(high_ref, low_ref, at, tiles):
        high, low = split(jnp.concatenate(tiles, axis=0))
        high_ref[at * 16 : (at + 1) * 16, :] = high.astype(jnp.bfloat16)
        low_ref[at * 16 : (at + 1) * 16, :] = low.astype(jnp.bfloat16)

    for pair in range(total // 16):
        store(all_high, all_low, pair, [arrived(2 * pair), arrived(2 * pair + 1)])

    upper_rows = lax.broadcasted_iota(jnp.int32, (8, stacked_ref.shape[1]), 0) < 4
    odd = quarter % 2 == 1

    def owned_tile(at):
        tiles = [arrived((slot ^ (SECOND_TURN // 4)) * 2 + quarter // 2) for slot in (at, at + 1)]
        turned = [pltpu.roll(tile, 4, 0) for tile in tiles]
        first = jnp.where(odd, turned[0], tiles[0])
        second = jnp.where(odd, tiles[1], turned[1])
        return jnp.where(upper_rows, first, second)

    for quad in range(8):
        store(own_high, own_low, quad, [owned_tile(4 * quad), owned_tile(4 * quad + 2)])
    contract = (((1,), (1,)), ((), ()))

    def multiply(one, other):
        return lax.dot_general(one, other, contract, preferred_element_type=jnp.float32)

    high, low = all_high[...], all_low[...]
    a_high, a_low = own_high[...], own_low[...]
    partial = multiply(a_high, high) + multiply(a_high, low) + multiply(a_low, high)
    partial = partial * scale
    count = partial.shape[0]
    pieces = total // BLOCK
    for piece in range(pieces):
        partial_ref[pl.ds(piece, count, stride=pieces), :] = partial[
            :, piece * BLOCK : (piece + 1) * BLOCK
        ]


def on_device(vectors, tile_table, offsets, tile_ids, bounds):
    vecs, local_rows = vectors.shape
    count = local_rows // BLOCK
    extent = count + 2 * HALO
    edge = HALO * BLOCK
    size = lax.axis_size(ROWS)
    up = [(i, i + 1) for i in range(size - 1)]
    down = [(j, i) for i, j in up]
    vmem = pl.BlockSpec(memory_space=pltpu.VMEM)
    smem = pl.BlockSpec(memory_space=pltpu.SMEM)
    hbm = pl.BlockSpec(memory_space=pltpu.HBM)
    packed = jax.ShapeDtypeStruct((vecs, edge + BLOCK), jnp.float32)
    slots = pltpu.VMEM((3, count), jnp.int32)
    to_upper, to_lower, meta, tiles = pl.pallas_call(
        pack_kernel,
        out_shape=(
            packed,
            packed,
            jax.ShapeDtypeStruct((8, BLOCK), jnp.float32),
            jax.ShapeDtypeStruct(tile_table.shape, jnp.float32),
        ),
        in_specs=[hbm] * 4,
        out_specs=(vmem,) * 4,
        scratch_shapes=[slots, slots, pltpu.SemaphoreType.DMA((5,))],
        compiler_params=pltpu.CompilerParams(vmem_limit_bytes=4 * MIB),
        name="pack",
    )(*(
        pltpu.with_memory_space_constraint(array, pltpu.HBM)
        for array in (vectors, offsets.T, tile_ids.T, tile_table)
    ))
    before = lax.ppermute(to_upper, ROWS, up)
    after = lax.ppermute(to_lower, ROWS, down)

    table = pl.pallas_call(
        table_kernel,
        out_shape=jax.ShapeDtypeStruct((3 * NT, BLOCK, 2 * BLOCK), jnp.bfloat16),
        in_specs=[vmem],
        out_specs=vmem,
        compiler_params=pltpu.CompilerParams(vmem_limit_bytes=16 * MIB),
        name="table",
    )(tiles)

    field = pltpu.VMEM((extent, vecs, BLOCK), jnp.float32)
    parts = pltpu.VMEM((extent, 2 * vecs, BLOCK), jnp.bfloat16)
    filtered, outgoing = pl.pallas_call(
        filter_kernel,
        out_shape=(
            jax.ShapeDtypeStruct((vecs, local_rows), jnp.float32),
            jax.ShapeDtypeStruct((64, vecs, 2 * BLOCK), jnp.float32),
        ),
        in_specs=[vmem, vmem, vmem, vmem, vmem, smem],
        out_specs=(vmem, vmem),
        scratch_shapes=[
            field, field, field, parts, parts,
            pltpu.VMEM((8, BLOCK), jnp.int32),
            pltpu.SMEM((8, BLOCK), jnp.int32),
            pltpu.SemaphoreType.DMA(()),
        ],
        compiler_params=pltpu.CompilerParams(vmem_limit_bytes=16 * MIB),
        name="filter",
    )(vectors, before, after, meta, table, bounds)

    stacked = lax.all_to_all(
        outgoing,
        VEC,
        split_axis=0,
        concat_axis=0,
        tiled=True,
        axis_index_groups=[[at ^ FIRST_TURN for at in range(64)]],
    )
    total = 64 * vecs
    stacked = stacked.reshape(total, 2 * BLOCK)
    owned = total // 4
    partial = pl.pallas_call(
        functools.partial(gram_kernel, 1.0 / (local_rows * size)),
        out_shape=jax.ShapeDtypeStruct((owned * (total // BLOCK), BLOCK), jnp.float32),
        in_specs=[vmem],
        out_specs=vmem,
        scratch_shapes=[pltpu.VMEM((total, 2 * BLOCK), jnp.bfloat16)] * 2
        + [pltpu.VMEM((owned, 2 * BLOCK), jnp.bfloat16)] * 2,
        compiler_params=pltpu.CompilerParams(vmem_limit_bytes=16 * MIB),
        name="gram",
    )(stacked)
    received = lax.all_to_all(
        partial.reshape(owned, 1, total),
        OWNERS,
        split_axis=0,
        concat_axis=0,
        tiled=True,
        axis_index_groups=[[at ^ SECOND_TURN for at in range(owned)]],
    )
    gram_matrix = jnp.sum(received, axis=0)
    return filtered, gram_matrix


def solution(mesh):
    fine = Mesh(mesh.devices.reshape(4, 2, 4, 4, 2, 2), ROWS + VEC)
    placed = (P(VEC, ROWS), P(), P(ROWS, None), P(ROWS, None), P())
    return jax.shard_map(
        on_device,
        mesh=fine,
        in_specs=placed,
        out_specs=(P(VEC, ROWS), P(ROWS + VEC, None)),
        check_vma=False,
    )
```

```python
import functools

import jax
import jax.numpy as jnp
from jax import lax
from jax.experimental import pallas as pl
from jax.experimental.pallas import tpu as pltpu
from jax.sharding import Mesh, PartitionSpec as P

BLOCK = 128
STEPS = 4
REACH = 2
HALO = STEPS * REACH
NT = 16
MIB = 1 << 20
ROWS = ("zl", "core")
VEC = ("x", "yq", "yb", "zh")
OWNERS = ROWS + ("x", "yb", "zh")
FIRST_TURN = 0b101001
SECOND_TURN = 0b1101000


def split(value):
    high = value.astype(jnp.bfloat16).astype(jnp.float32)
    return high, value - high


def table_kernel(tiles_ref, table_ref, tiles_here, sems):
    step = NT // sems.shape[0]
    copies = [
        pltpu.make_async_copy(
            tiles_ref.at[at : at + step], tiles_here.at[at : at + step], sems.at[at // step]
        )
        for at in range(0, NT, step)
    ]
    for copy in copies:
        copy.start()
    for tile in range(NT):
        if tile % step == 0:
            copies[tile // step].wait()
        straight = tiles_here[tile]
        flipped = straight.T
        for kind, matrix in enumerate((flipped, straight, (straight + flipped) / 2)):
            high, low = split(matrix)
            entry = tile + NT * kind
            table_ref[entry, :, :BLOCK] = high.astype(jnp.bfloat16)
            table_ref[entry, :, BLOCK:] = low.astype(jnp.bfloat16)


def pack_kernel(
    vectors_ref, offsets_ref, ids_ref, mate_ref, cross_ref, own_ref, offsets_here, ids_here, sems
):
    edge = mate_ref.shape[1] - BLOCK
    last = vectors_ref.shape[1] - edge
    core = lax.axis_index("core")
    to_mate = pl.ds(pl.multiple_of((1 - core) * last, BLOCK), edge)
    to_cross = pl.ds(pl.multiple_of(core * last, BLOCK), edge)
    slots, count = offsets_ref.shape
    copies = [
        pltpu.make_async_copy(source, target, sems.at[at])
        for at, (source, target) in enumerate(
            (
                (offsets_ref, offsets_here),
                (ids_ref, ids_here),
                (vectors_ref.at[:, to_mate], mate_ref.at[:, :edge]),
                (vectors_ref.at[:, to_cross], cross_ref.at[:, :edge]),
            )
        )
    ]
    for copy in copies:
        copy.start()
    own_ref[...] = jnp.zeros_like(own_ref)
    copies[0].wait()
    copies[1].wait()
    own_ref[:slots, :count] = offsets_here[...].astype(jnp.float32)
    own_ref[slots : 2 * slots, :count] = ids_here[...].astype(jnp.float32)
    mate_ref[:, edge:] = own_ref[...]
    cross_ref[:, edge:] = own_ref[...]
    copies[2].wait()
    copies[3].wait()


def filter_kernel(
    vectors_ref, mate_ref, cross_ref, own_ref, table_ref, bounds_ref,
    filtered_ref, outgoing_ref,
    field_a, field_b, field_c, parts_a, parts_b, plan_vector, plan, sem,
):
    vecs = vectors_ref.shape[0]
    count = vectors_ref.shape[1] // BLOCK
    extent = count + 2 * HALO
    edge = HALO * BLOCK

    upper = lax.axis_index("core") == 1

    def before(at):
        return jnp.where(upper, mate_ref[:, at], cross_ref[:, at])

    def after(at):
        return jnp.where(upper, cross_ref[:, at], mate_ref[:, at])

    last = slice(edge, edge + BLOCK)
    lane = lax.broadcasted_iota(jnp.int32, (8, 128), 1)
    row = lax.broadcasted_iota(jnp.int32, (8, 128), 0)
    left = pltpu.roll(before(last), 128 - (count - HALO), 1)
    own = pltpu.roll(own_ref[...], HALO, 1)
    right = pltpu.roll(after(last), HALO + count, 1)
    meta = jnp.where(lane < HALO, left, jnp.where(lane < HALO + count, own, right))
    meta = meta.astype(jnp.int32)
    shift = pltpu.roll(meta, 3, 0)
    kind = jnp.where(shift > 0, 0, jnp.where(shift < 0, NT, 2 * NT))
    plan_vector[...] = jnp.where(row < 3, meta + lane, meta + kind)
    copy = pltpu.make_async_copy(plan_vector, plan, sem)
    copy.start()

    def store_parts(target, block, value):
        high, low = split(value)
        target[block] = jnp.concatenate([high, low], axis=0).astype(jnp.bfloat16)

    for block in range(extent):
        if block < HALO:
            value = before(slice(block * BLOCK, (block + 1) * BLOCK))
        elif block < HALO + count:
            at = (block - HALO) * BLOCK
            value = vectors_ref[:, at : at + BLOCK]
        else:
            at = (block - HALO - count) * BLOCK
            value = after(slice(at, at + BLOCK))
        field_a[block] = value
        store_parts(parts_a, block, value)

    lowest, low_end, high_end = bounds_ref[0], bounds_ref[1], bounds_ref[2]

    def spread(value):
        return jnp.full((vecs, BLOCK), value, jnp.float32)

    half_width = spread((high_end - low_end) * 0.5)
    centre = spread((high_end + low_end) * 0.5)
    sigma_one = half_width / (spread(lowest) - centre)
    sigma_base = 2 / sigma_one
    copy.wait()

    def product(parts, block):
        left_parts, right_parts = [], []
        for slot in range(3):
            left_parts.append(parts[plan[slot, block]])
            right_parts.append(table_ref[plan[3 + slot, block]])
        both = lax.dot_general(
            jnp.concatenate(left_parts, axis=1),
            jnp.concatenate(right_parts, axis=0),
            (((1,), (0,)), ((), ())),
            preferred_element_type=jnp.float32,
        )
        return both[:vecs, :BLOCK] + both[vecs:, :BLOCK] + both[:vecs, BLOCK:]

    fields = [field_a, field_b, field_c, field_a]
    parts = [parts_a, parts_b, parts_a, parts_b]
    sigma = sigma_one
    for step in range(1, STEPS + 1):
        source, source_parts = fields[step - 1], parts[step - 1]
        if step == 1:
            scale, drag = sigma_one / half_width, None
        else:
            following = 1 / (sigma_base - sigma)
            scale, drag = 2 * following / half_width, sigma * following
            sigma = following
        first = REACH * step

        def one_block(block, owner, part):
            value = scale * (product(source_parts, block) - centre * source[block])
            if drag is not None:
                value = value - drag * fields[step - 2][block]
            if step < STEPS:
                fields[step][block] = value
                store_parts(parts[step], block, value)
            else:
                at = block - HALO
                filtered_ref[:, pl.ds(pl.multiple_of(at * BLOCK, BLOCK), BLOCK)] = value
                upper, lower = owner
                for quarter in range(4):
                    inner = (lower // 4 * 16 + quarter * 4 + lower % 4) ^ (FIRST_TURN % 32)
                    outgoing_ref[
                        (upper ^ (FIRST_TURN // 32)) * 32 + inner,
                        :,
                        part * BLOCK : (part + 1) * BLOCK,
                    ] = value

        group = (extent - 2 * first) // 2

        @pl.loop(0, 2)
        def _(index):
            for inner in range(group):
                one_block(first + index * group + inner, (index, inner // 2), inner % 2)


def gram_kernel(scale, stacked_ref, partial_ref, all_high, all_low, own_high, own_low):
    total = stacked_ref.shape[0]
    quarter = lax.axis_index("yq")

    def arrived(at):
        return stacked_ref[pl.ds(pl.multiple_of((at ^ FIRST_TURN) * 8, 8), 8), :]

    def store(high_ref, low_ref, at, tiles):
        high, low = split(jnp.concatenate(tiles, axis=0))
        high_ref[at * 16 : (at + 1) * 16, :] = high.astype(jnp.bfloat16)
        low_ref[at * 16 : (at + 1) * 16, :] = low.astype(jnp.bfloat16)

    for pair in range(total // 16):
        store(all_high, all_low, pair, [arrived(2 * pair), arrived(2 * pair + 1)])

    upper_rows = lax.broadcasted_iota(jnp.int32, (8, stacked_ref.shape[1]), 0) < 4
    odd = quarter % 2 == 1

    row = lax.broadcasted_iota(jnp.int32, (8, stacked_ref.shape[1]), 0)

    def turned_rows(tile):
        for bit in (1, 2):
            if SECOND_TURN & bit:
                back, forth = pltpu.roll(tile, 8 - bit, 0), pltpu.roll(tile, bit, 0)
                tile = jnp.where(row & bit == 0, back, forth)
        return tile

    def owned_tile(at):
        tiles = [arrived((slot ^ (SECOND_TURN // 4)) * 2 + quarter // 2) for slot in (at, at + 1)]
        turned = [pltpu.roll(tile, 4, 0) for tile in tiles]
        first = jnp.where(odd, turned[0], tiles[0])
        second = jnp.where(odd, tiles[1], turned[1])
        return turned_rows(jnp.where(upper_rows, first, second))

    for quad in range(8):
        store(own_high, own_low, quad, [owned_tile(4 * quad), owned_tile(4 * quad + 2)])
    contract = (((1,), (1,)), ((), ()))

    def multiply(one, other):
        return lax.dot_general(one, other, contract, preferred_element_type=jnp.float32)

    high, low = all_high[...], all_low[...]
    a_high, a_low = own_high[...], own_low[...]
    partial = multiply(a_high, high) + multiply(a_high, low) + multiply(a_low, high)
    partial = partial * scale
    count = partial.shape[0]
    pieces = total // BLOCK
    for piece in range(pieces):
        partial_ref[pl.ds(piece, count, stride=pieces), :] = partial[
            :, piece * BLOCK : (piece + 1) * BLOCK
        ]


def on_device(vectors, tile_table, offsets, tile_ids, bounds):
    vecs, local_rows = vectors.shape
    count = local_rows // BLOCK
    extent = count + 2 * HALO
    edge = HALO * BLOCK
    size = lax.axis_size(ROWS)
    mates = [(i, i ^ 1) for i in range(size)]
    across = [(i, i + 1 if i % 2 else i - 1) for i in range(1, size - 1)]
    vmem = pl.BlockSpec(memory_space=pltpu.VMEM)
    smem = pl.BlockSpec(memory_space=pltpu.SMEM)
    hbm = pl.BlockSpec(memory_space=pltpu.HBM)
    packed = jax.ShapeDtypeStruct((vecs, edge + BLOCK), jnp.float32)
    slots = pltpu.VMEM((3, count), jnp.int32)
    to_mate, to_cross, meta = pl.pallas_call(
        pack_kernel,
        out_shape=(packed, packed, jax.ShapeDtypeStruct((8, BLOCK), jnp.float32)),
        in_specs=[hbm, hbm, hbm],
        out_specs=(vmem, vmem, vmem),
        scratch_shapes=[slots, slots, pltpu.SemaphoreType.DMA((4,))],
        compiler_params=pltpu.CompilerParams(vmem_limit_bytes=4 * MIB),
        name="pack",
    )(*(
        pltpu.with_memory_space_constraint(array, pltpu.HBM)
        for array in (vectors, offsets.T, tile_ids.T)
    ))
    cross = lax.ppermute(to_cross, ROWS, across)
    mate = lax.ppermute(to_mate, ROWS, mates)

    table = pl.pallas_call(
        table_kernel,
        out_shape=jax.ShapeDtypeStruct((3 * NT, BLOCK, 2 * BLOCK), jnp.bfloat16),
        in_specs=[hbm],
        out_specs=vmem,
        scratch_shapes=[
            pltpu.VMEM(tile_table.shape, jnp.float32),
            pltpu.SemaphoreType.DMA((4,)),
        ],
        compiler_params=pltpu.CompilerParams(vmem_limit_bytes=16 * MIB),
        name="table",
    )(pltpu.with_memory_space_constraint(tile_table, pltpu.HBM))

    field = pltpu.VMEM((extent, vecs, BLOCK), jnp.float32)
    parts = pltpu.VMEM((extent, 2 * vecs, BLOCK), jnp.bfloat16)
    filtered, outgoing = pl.pallas_call(
        filter_kernel,
        out_shape=(
            jax.ShapeDtypeStruct((vecs, local_rows), jnp.float32),
            jax.ShapeDtypeStruct((64, vecs, 2 * BLOCK), jnp.float32),
        ),
        in_specs=[vmem, vmem, vmem, vmem, vmem, smem],
        out_specs=(vmem, vmem),
        scratch_shapes=[
            field, field, field, parts, parts,
            pltpu.VMEM((8, BLOCK), jnp.int32),
            pltpu.SMEM((8, BLOCK), jnp.int32),
            pltpu.SemaphoreType.DMA(()),
        ],
        compiler_params=pltpu.CompilerParams(vmem_limit_bytes=16 * MIB),
        name="filter",
    )(vectors, mate, cross, meta, table, bounds)

    stacked = lax.all_to_all(
        outgoing,
        VEC,
        split_axis=0,
        concat_axis=0,
        tiled=True,
        axis_index_groups=[[at ^ FIRST_TURN for at in range(64)]],
    )
    total = 64 * vecs
    stacked = stacked.reshape(total, 2 * BLOCK)
    owned = total // 4
    partial = pl.pallas_call(
        functools.partial(gram_kernel, 1.0 / (local_rows * size)),
        out_shape=jax.ShapeDtypeStruct((owned * (total // BLOCK), BLOCK), jnp.float32),
        in_specs=[vmem],
        out_specs=vmem,
        scratch_shapes=[pltpu.VMEM((total, 2 * BLOCK), jnp.bfloat16)] * 2
        + [pltpu.VMEM((owned, 2 * BLOCK), jnp.bfloat16)] * 2,
        compiler_params=pltpu.CompilerParams(vmem_limit_bytes=16 * MIB),
        name="gram",
    )(stacked)
    received = lax.all_to_all(
        partial.reshape(owned, 1, total),
        OWNERS,
        split_axis=0,
        concat_axis=0,
        tiled=True,
        axis_index_groups=[[at ^ SECOND_TURN for at in range(owned)]],
    )
    gram_matrix = jnp.sum(received, axis=0)
    return filtered, gram_matrix


def solution(mesh):
    fine = Mesh(mesh.devices.reshape(4, 2, 4, 4, 2, 2), ROWS + VEC)
    placed = (P(VEC, ROWS), P(), P(ROWS, None), P(ROWS, None), P())
    return jax.shard_map(
        on_device,
        mesh=fine,
        in_specs=placed,
        out_specs=(P(VEC, ROWS), P(ROWS + VEC, None)),
        check_vma=False,
    )
```

```python
import functools

import jax
import jax.numpy as jnp
from jax import lax
from jax.experimental import pallas as pl
from jax.experimental.pallas import tpu as pltpu
from jax.sharding import Mesh, PartitionSpec as P

BLOCK = 128
STEPS = 4
REACH = 2
HALO = STEPS * REACH
NT = 16
MIB = 1 << 20
ROWS = ("zl", "core")
VEC = ("x", "yq", "yb", "zh")
OWNERS = ROWS + ("x", "yb", "zh")
FIRST_TURN = 0b101001
SECOND_TURN = 0b1101001


def split(value):
    high = value.astype(jnp.bfloat16).astype(jnp.float32)
    return high, value - high


def table_kernel(tiles_ref, table_ref, tiles_here, sems):
    step = NT // sems.shape[0]
    copies = [
        pltpu.make_async_copy(
            tiles_ref.at[at : at + step], tiles_here.at[at : at + step], sems.at[at // step]
        )
        for at in range(0, NT, step)
    ]
    for copy in copies:
        copy.start()
    for tile in range(NT):
        if tile % step == 0:
            copies[tile // step].wait()
        straight = tiles_here[tile]
        flipped = straight.T
        for kind, matrix in enumerate((flipped, straight, (straight + flipped) / 2)):
            high, low = split(matrix)
            entry = tile + NT * kind
            table_ref[entry, :, :BLOCK] = high.astype(jnp.bfloat16)
            table_ref[entry, :, BLOCK:] = low.astype(jnp.bfloat16)


def pack_kernel(
    vectors_ref, offsets_ref, ids_ref, mate_ref, cross_ref, own_ref, offsets_here, ids_here, sems
):
    edge = mate_ref.shape[1] - BLOCK
    last = vectors_ref.shape[1] - edge
    core = lax.axis_index("core")
    to_mate = pl.ds(pl.multiple_of((1 - core) * last, BLOCK), edge)
    to_cross = pl.ds(pl.multiple_of(core * last, BLOCK), edge)
    slots, count = offsets_ref.shape
    copies = [
        pltpu.make_async_copy(source, target, sems.at[at])
        for at, (source, target) in enumerate(
            (
                (offsets_ref, offsets_here),
                (ids_ref, ids_here),
                (vectors_ref.at[:, to_mate], mate_ref.at[:, :edge]),
                (vectors_ref.at[:, to_cross], cross_ref.at[:, :edge]),
            )
        )
    ]
    for copy in copies:
        copy.start()
    own_ref[...] = jnp.zeros_like(own_ref)
    copies[0].wait()
    copies[1].wait()
    own_ref[:slots, :count] = offsets_here[...].astype(jnp.float32)
    own_ref[slots : 2 * slots, :count] = ids_here[...].astype(jnp.float32)
    mate_ref[:, edge:] = own_ref[...]
    cross_ref[:, edge:] = own_ref[...]
    copies[2].wait()
    copies[3].wait()


def filter_kernel(
    vectors_ref, mate_ref, cross_ref, own_ref, table_ref, bounds_ref,
    filtered_ref, outgoing_ref,
    field_a, field_b, field_c, parts_a, parts_b, plan_vector, plan, sem,
):
    vecs = vectors_ref.shape[0]
    count = vectors_ref.shape[1] // BLOCK
    extent = count + 2 * HALO
    edge = HALO * BLOCK

    upper = lax.axis_index("core") == 1

    def before(at):
        return jnp.where(upper, mate_ref[:, at], cross_ref[:, at])

    def after(at):
        return jnp.where(upper, cross_ref[:, at], mate_ref[:, at])

    last = slice(edge, edge + BLOCK)
    lane = lax.broadcasted_iota(jnp.int32, (8, 128), 1)
    row = lax.broadcasted_iota(jnp.int32, (8, 128), 0)
    left = pltpu.roll(before(last), 128 - (count - HALO), 1)
    own = pltpu.roll(own_ref[...], HALO, 1)
    right = pltpu.roll(after(last), HALO + count, 1)
    meta = jnp.where(lane < HALO, left, jnp.where(lane < HALO + count, own, right))
    meta = meta.astype(jnp.int32)
    shift = pltpu.roll(meta, 3, 0)
    kind = jnp.where(shift > 0, 0, jnp.where(shift < 0, NT, 2 * NT))
    plan_vector[...] = jnp.where(row < 3, meta + lane, meta + kind)
    copy = pltpu.make_async_copy(plan_vector, plan, sem)
    copy.start()

    def store_parts(target, block, value):
        high, low = split(value)
        target[block] = jnp.concatenate([high, low], axis=0).astype(jnp.bfloat16)

    for block in range(extent):
        if block < HALO:
            value = before(slice(block * BLOCK, (block + 1) * BLOCK))
        elif block < HALO + count:
            at = (block - HALO) * BLOCK
            value = vectors_ref[:, at : at + BLOCK]
        else:
            at = (block - HALO - count) * BLOCK
            value = after(slice(at, at + BLOCK))
        field_a[block] = value
        store_parts(parts_a, block, value)

    lowest, low_end, high_end = bounds_ref[0], bounds_ref[1], bounds_ref[2]

    def spread(value):
        return jnp.full((vecs, BLOCK), value, jnp.float32)

    half_width = spread((high_end - low_end) * 0.5)
    centre = spread((high_end + low_end) * 0.5)
    sigma_one = half_width / (spread(lowest) - centre)
    sigma_base = 2 / sigma_one
    copy.wait()

    def product(parts, block):
        left_parts, right_parts = [], []
        for slot in range(3):
            left_parts.append(parts[plan[slot, block]])
            right_parts.append(table_ref[plan[3 + slot, block]])
        both = lax.dot_general(
            jnp.concatenate(left_parts, axis=1),
            jnp.concatenate(right_parts, axis=0),
            (((1,), (0,)), ((), ())),
            preferred_element_type=jnp.float32,
        )
        return both[:vecs, :BLOCK] + both[vecs:, :BLOCK] + both[:vecs, BLOCK:]

    fields = [field_a, field_b, field_c, field_a]
    parts = [parts_a, parts_b, parts_a, parts_b]
    sigma = sigma_one
    for step in range(1, STEPS + 1):
        source, source_parts = fields[step - 1], parts[step - 1]
        if step == 1:
            scale, drag = sigma_one / half_width, None
        else:
            following = 1 / (sigma_base - sigma)
            scale, drag = 2 * following / half_width, sigma * following
            sigma = following
        first = REACH * step

        def one_block(block, owner, part):
            value = scale * (product(source_parts, block) - centre * source[block])
            if drag is not None:
                value = value - drag * fields[step - 2][block]
            if step < STEPS:
                fields[step][block] = value
                store_parts(parts[step], block, value)
            else:
                at = block - HALO
                filtered_ref[:, pl.ds(pl.multiple_of(at * BLOCK, BLOCK), BLOCK)] = value
                upper, lower = owner
                for quarter in range(4):
                    inner = (lower // 4 * 16 + quarter * 4 + lower % 4) ^ (FIRST_TURN % 32)
                    outgoing_ref[
                        (upper ^ (FIRST_TURN // 32)) * 32 + inner,
                        :,
                        part * BLOCK : (part + 1) * BLOCK,
                    ] = value

        group = (extent - 2 * first) // 2

        @pl.loop(0, 2)
        def _(index):
            for inner in range(group):
                one_block(first + index * group + inner, (index, inner // 2), inner % 2)


def gram_kernel(
    scale, stacked_ref, filtered_ref, partial_ref, kept_ref,
    all_high, all_low, own_high, own_low, sem,
):
    keep = pltpu.make_async_copy(filtered_ref, kept_ref, sem)
    keep.start()
    total = stacked_ref.shape[0]
    quarter = lax.axis_index("yq")

    def arrived(at):
        return stacked_ref[pl.ds(pl.multiple_of((at ^ FIRST_TURN) * 8, 8), 8), :]

    def store(high_ref, low_ref, at, tiles):
        high, low = split(jnp.concatenate(tiles, axis=0))
        high_ref[at * 16 : (at + 1) * 16, :] = high.astype(jnp.bfloat16)
        low_ref[at * 16 : (at + 1) * 16, :] = low.astype(jnp.bfloat16)

    for pair in range(total // 16):
        store(all_high, all_low, pair, [arrived(2 * pair), arrived(2 * pair + 1)])

    upper_rows = lax.broadcasted_iota(jnp.int32, (8, stacked_ref.shape[1]), 0) < 4
    odd = quarter % 2 == 1

    row = lax.broadcasted_iota(jnp.int32, (8, stacked_ref.shape[1]), 0)

    def turned_rows(tile):
        for bit in (1, 2):
            if SECOND_TURN & bit:
                back, forth = pltpu.roll(tile, 8 - bit, 0), pltpu.roll(tile, bit, 0)
                tile = jnp.where(row & bit == 0, back, forth)
        return tile

    def owned_tile(at):
        tiles = [arrived((slot ^ (SECOND_TURN // 4)) * 2 + quarter // 2) for slot in (at, at + 1)]
        turned = [pltpu.roll(tile, 4, 0) for tile in tiles]
        first = jnp.where(odd, turned[0], tiles[0])
        second = jnp.where(odd, tiles[1], turned[1])
        return turned_rows(jnp.where(upper_rows, first, second))

    for quad in range(8):
        store(own_high, own_low, quad, [owned_tile(4 * quad), owned_tile(4 * quad + 2)])
    contract = (((1,), (1,)), ((), ()))

    def multiply(one, other):
        return lax.dot_general(one, other, contract, preferred_element_type=jnp.float32)

    high, low = all_high[...], all_low[...]
    a_high, a_low = own_high[...], own_low[...]
    partial = multiply(a_high, high) + multiply(a_high, low) + multiply(a_low, high)
    partial = partial * scale
    count = partial.shape[0]
    pieces = total // BLOCK
    for piece in range(pieces):
        partial_ref[pl.ds(piece, count, stride=pieces), :] = partial[
            :, piece * BLOCK : (piece + 1) * BLOCK
        ]
    keep.wait()


def on_device(vectors, tile_table, offsets, tile_ids, bounds):
    vecs, local_rows = vectors.shape
    count = local_rows // BLOCK
    extent = count + 2 * HALO
    edge = HALO * BLOCK
    size = lax.axis_size(ROWS)
    mates = [(i, i ^ 1) for i in range(size)]
    across = [(i, i + 1 if i % 2 else i - 1) for i in range(1, size - 1)]
    vmem = pl.BlockSpec(memory_space=pltpu.VMEM)
    smem = pl.BlockSpec(memory_space=pltpu.SMEM)
    hbm = pl.BlockSpec(memory_space=pltpu.HBM)
    packed = jax.ShapeDtypeStruct((vecs, edge + BLOCK), jnp.float32)
    slots = pltpu.VMEM((3, count), jnp.int32)
    to_mate, to_cross, meta = pl.pallas_call(
        pack_kernel,
        out_shape=(packed, packed, jax.ShapeDtypeStruct((8, BLOCK), jnp.float32)),
        in_specs=[hbm, hbm, hbm],
        out_specs=(vmem, vmem, vmem),
        scratch_shapes=[slots, slots, pltpu.SemaphoreType.DMA((4,))],
        compiler_params=pltpu.CompilerParams(vmem_limit_bytes=4 * MIB),
        name="pack",
    )(*(
        pltpu.with_memory_space_constraint(array, pltpu.HBM)
        for array in (vectors, offsets.T, tile_ids.T)
    ))
    cross = lax.ppermute(to_cross, ROWS, across)
    mate = lax.ppermute(to_mate, ROWS, mates)

    table = pl.pallas_call(
        table_kernel,
        out_shape=jax.ShapeDtypeStruct((3 * NT, BLOCK, 2 * BLOCK), jnp.bfloat16),
        in_specs=[hbm],
        out_specs=vmem,
        scratch_shapes=[
            pltpu.VMEM(tile_table.shape, jnp.float32),
            pltpu.SemaphoreType.DMA((4,)),
        ],
        compiler_params=pltpu.CompilerParams(vmem_limit_bytes=16 * MIB),
        name="table",
    )(pltpu.with_memory_space_constraint(tile_table, pltpu.HBM))

    field = pltpu.VMEM((extent, vecs, BLOCK), jnp.float32)
    parts = pltpu.VMEM((extent, 2 * vecs, BLOCK), jnp.bfloat16)
    filtered, outgoing = pl.pallas_call(
        filter_kernel,
        out_shape=(
            pltpu.VMEM((vecs, local_rows), jnp.float32),
            jax.ShapeDtypeStruct((64, vecs, 2 * BLOCK), jnp.float32),
        ),
        in_specs=[vmem, vmem, vmem, vmem, vmem, smem],
        out_specs=(vmem, vmem),
        scratch_shapes=[
            field, field, field, parts, parts,
            pltpu.VMEM((8, BLOCK), jnp.int32),
            pltpu.SMEM((8, BLOCK), jnp.int32),
            pltpu.SemaphoreType.DMA(()),
        ],
        compiler_params=pltpu.CompilerParams(vmem_limit_bytes=16 * MIB),
        name="filter",
    )(vectors, mate, cross, meta, table, bounds)

    stacked = lax.all_to_all(
        outgoing,
        VEC,
        split_axis=0,
        concat_axis=0,
        tiled=True,
        axis_index_groups=[[at ^ FIRST_TURN for at in range(64)]],
    )
    total = 64 * vecs
    stacked = stacked.reshape(total, 2 * BLOCK)
    owned = total // 4
    partial, kept = pl.pallas_call(
        functools.partial(gram_kernel, 1.0 / (local_rows * size)),
        out_shape=(
            jax.ShapeDtypeStruct((owned * (total // BLOCK), BLOCK), jnp.float32),
            jax.ShapeDtypeStruct(filtered.shape, jnp.float32),
        ),
        in_specs=[vmem, vmem],
        out_specs=(vmem, hbm),
        scratch_shapes=[pltpu.VMEM((total, 2 * BLOCK), jnp.bfloat16)] * 2
        + [pltpu.VMEM((owned, 2 * BLOCK), jnp.bfloat16)] * 2
        + [pltpu.SemaphoreType.DMA(())],
        compiler_params=pltpu.CompilerParams(vmem_limit_bytes=16 * MIB),
        name="gram",
    )(stacked, filtered)
    received = lax.all_to_all(
        partial.reshape(owned, 1, total),
        OWNERS,
        split_axis=0,
        concat_axis=0,
        tiled=True,
        axis_index_groups=[[at ^ SECOND_TURN for at in range(owned)]],
    )
    gram_matrix = jnp.sum(received, axis=0)
    return kept, gram_matrix


def solution(mesh):
    fine = Mesh(mesh.devices.reshape(4, 2, 4, 4, 2, 2), ROWS + VEC)
    placed = (P(VEC, ROWS), P(), P(ROWS, None), P(ROWS, None), P())
    return jax.shard_map(
        on_device,
        mesh=fine,
        in_specs=placed,
        out_specs=(P(VEC, ROWS), P(ROWS + VEC, None)),
        check_vma=False,
    )
```

```python
import functools

import jax
import jax.numpy as jnp
from jax import lax
from jax.experimental import pallas as pl
from jax.experimental.pallas import tpu as pltpu
from jax.sharding import Mesh, PartitionSpec as P

BLOCK = 128
STEPS = 4
REACH = 2
HALO = STEPS * REACH
NT = 16
MIB = 1 << 20
ROWS = ("zl", "core")
VEC = ("x", "yq", "yb", "zh")
OWNERS = ROWS + ("x", "yb", "zh")
FIRST_TURN = 0b101011
SECOND_TURN = 0b1111001


def split(value):
    high = value.astype(jnp.bfloat16).astype(jnp.float32)
    return high, value - high


def table_kernel(tiles_ref, table_ref, tiles_here, sems):
    step = NT // sems.shape[0]
    copies = [
        pltpu.make_async_copy(
            tiles_ref.at[at : at + step], tiles_here.at[at : at + step], sems.at[at // step]
        )
        for at in range(0, NT, step)
    ]
    for copy in copies:
        copy.start()
    for tile in range(NT):
        if tile % step == 0:
            copies[tile // step].wait()
        straight = tiles_here[tile]
        flipped = straight.T
        for kind, matrix in enumerate((flipped, straight, (straight + flipped) / 2)):
            high, low = split(matrix)
            entry = tile + NT * kind
            table_ref[entry, :, :BLOCK] = high.astype(jnp.bfloat16)
            table_ref[entry, :, BLOCK:] = low.astype(jnp.bfloat16)


def pack_kernel(
    vectors_ref, offsets_ref, ids_ref, mate_ref, cross_ref, own_ref, offsets_here, ids_here, sems
):
    edge = mate_ref.shape[1] - BLOCK
    last = vectors_ref.shape[1] - edge
    core = lax.axis_index("core")
    to_mate = pl.ds(pl.multiple_of((1 - core) * last, BLOCK), edge)
    to_cross = pl.ds(pl.multiple_of(core * last, BLOCK), edge)
    slots, count = offsets_ref.shape
    copies = [
        pltpu.make_async_copy(source, target, sems.at[at])
        for at, (source, target) in enumerate(
            (
                (offsets_ref, offsets_here),
                (ids_ref, ids_here),
                (vectors_ref.at[:, to_mate], mate_ref.at[:, :edge]),
                (vectors_ref.at[:, to_cross], cross_ref.at[:, :edge]),
            )
        )
    ]
    for copy in copies:
        copy.start()
    own_ref[...] = jnp.zeros_like(own_ref)
    copies[0].wait()
    copies[1].wait()
    own_ref[:slots, :count] = offsets_here[...].astype(jnp.float32)
    own_ref[slots : 2 * slots, :count] = ids_here[...].astype(jnp.float32)
    mate_ref[:, edge:] = own_ref[...]
    cross_ref[:, edge:] = own_ref[...]
    copies[2].wait()
    copies[3].wait()


def filter_kernel(
    vectors_ref, mate_ref, cross_ref, own_ref, table_ref, bounds_ref,
    filtered_ref, outgoing_ref,
    field_a, field_b, field_c, parts_a, parts_b, plan_vector, plan, sem,
):
    vecs = vectors_ref.shape[0]
    count = vectors_ref.shape[1] // BLOCK
    extent = count + 2 * HALO
    edge = HALO * BLOCK

    upper = lax.axis_index("core") == 1

    def before(at):
        return jnp.where(upper, mate_ref[:, at], cross_ref[:, at])

    def after(at):
        return jnp.where(upper, cross_ref[:, at], mate_ref[:, at])

    last = slice(edge, edge + BLOCK)
    lane = lax.broadcasted_iota(jnp.int32, (8, 128), 1)
    row = lax.broadcasted_iota(jnp.int32, (8, 128), 0)
    left = pltpu.roll(before(last), 128 - (count - HALO), 1)
    own = pltpu.roll(own_ref[...], HALO, 1)
    right = pltpu.roll(after(last), HALO + count, 1)
    meta = jnp.where(lane < HALO, left, jnp.where(lane < HALO + count, own, right))
    meta = meta.astype(jnp.int32)
    shift = pltpu.roll(meta, 3, 0)
    kind = jnp.where(shift > 0, 0, jnp.where(shift < 0, NT, 2 * NT))
    plan_vector[...] = jnp.where(row < 3, meta + lane, meta + kind)
    copy = pltpu.make_async_copy(plan_vector, plan, sem)
    copy.start()

    def store_parts(target, block, value):
        high, low = split(value)
        target[block] = jnp.concatenate([high, low], axis=0).astype(jnp.bfloat16)

    for block in range(extent):
        if block < HALO:
            value = before(slice(block * BLOCK, (block + 1) * BLOCK))
        elif block < HALO + count:
            at = (block - HALO) * BLOCK
            value = vectors_ref[:, at : at + BLOCK]
        else:
            at = (block - HALO - count) * BLOCK
            value = after(slice(at, at + BLOCK))
        field_a[block] = value
        store_parts(parts_a, block, value)

    lowest, low_end, high_end = bounds_ref[0], bounds_ref[1], bounds_ref[2]

    def spread(value):
        return jnp.full((vecs, BLOCK), value, jnp.float32)

    half_width = spread((high_end - low_end) * 0.5)
    centre = spread((high_end + low_end) * 0.5)
    sigma_one = half_width / (spread(lowest) - centre)
    sigma_base = 2 / sigma_one
    copy.wait()

    def product(parts, block):
        left_parts, right_parts = [], []
        for slot in range(3):
            left_parts.append(parts[plan[slot, block]])
            right_parts.append(table_ref[plan[3 + slot, block]])
        both = lax.dot_general(
            jnp.concatenate(left_parts, axis=1),
            jnp.concatenate(right_parts, axis=0),
            (((1,), (0,)), ((), ())),
            preferred_element_type=jnp.float32,
        )
        return both[:vecs, :BLOCK] + both[vecs:, :BLOCK] + both[:vecs, BLOCK:]

    fields = [field_a, field_b, field_c, field_a]
    parts = [parts_a, parts_b, parts_a, parts_b]
    sigma = sigma_one
    for step in range(1, STEPS + 1):
        source, source_parts = fields[step - 1], parts[step - 1]
        if step == 1:
            scale, drag = sigma_one / half_width, None
        else:
            following = 1 / (sigma_base - sigma)
            scale, drag = 2 * following / half_width, sigma * following
            sigma = following
        first = REACH * step

        def one_block(block, owner, part):
            value = scale * (product(source_parts, block) - centre * source[block])
            if drag is not None:
                value = value - drag * fields[step - 2][block]
            if step < STEPS:
                fields[step][block] = value
                store_parts(parts[step], block, value)
            else:
                at = block - HALO
                filtered_ref[:, pl.ds(pl.multiple_of(at * BLOCK, BLOCK), BLOCK)] = value
                upper, lower = owner
                for quarter in range(4):
                    inner = (lower // 4 * 16 + quarter * 4 + lower % 4) ^ (FIRST_TURN % 32)
                    outgoing_ref[
                        (upper ^ (FIRST_TURN // 32)) * 32 + inner,
                        :,
                        part * BLOCK : (part + 1) * BLOCK,
                    ] = value

        group = (extent - 2 * first) // 2

        @pl.loop(0, 2)
        def _(index):
            for inner in range(group):
                one_block(first + index * group + inner, (index, inner // 2), inner % 2)


def gram_kernel(
    scale, stacked_ref, filtered_ref, partial_ref, kept_ref,
    all_high, all_low, own_high, own_low, sem,
):
    keep = pltpu.make_async_copy(filtered_ref, kept_ref, sem)
    keep.start()
    total = stacked_ref.shape[0]
    quarter = lax.axis_index("yq")

    def arrived(at):
        return stacked_ref[pl.ds(pl.multiple_of((at ^ FIRST_TURN) * 8, 8), 8), :]

    def store(high_ref, low_ref, at, tiles):
        high, low = split(jnp.concatenate(tiles, axis=0))
        high_ref[at * 16 : (at + 1) * 16, :] = high.astype(jnp.bfloat16)
        low_ref[at * 16 : (at + 1) * 16, :] = low.astype(jnp.bfloat16)

    for pair in range(total // 16):
        store(all_high, all_low, pair, [arrived(2 * pair), arrived(2 * pair + 1)])

    upper_rows = lax.broadcasted_iota(jnp.int32, (8, stacked_ref.shape[1]), 0) < 4
    odd = quarter % 2 == 1

    row = lax.broadcasted_iota(jnp.int32, (8, stacked_ref.shape[1]), 0)

    def turned_rows(tile):
        for bit in (1, 2):
            if SECOND_TURN & bit:
                back, forth = pltpu.roll(tile, 8 - bit, 0), pltpu.roll(tile, bit, 0)
                tile = jnp.where(row & bit == 0, back, forth)
        return tile

    def owned_tile(at):
        tiles = [arrived((slot ^ (SECOND_TURN // 4)) * 2 + quarter // 2) for slot in (at, at + 1)]
        turned = [pltpu.roll(tile, 4, 0) for tile in tiles]
        first = jnp.where(odd, turned[0], tiles[0])
        second = jnp.where(odd, tiles[1], turned[1])
        return turned_rows(jnp.where(upper_rows, first, second))

    for quad in range(8):
        store(own_high, own_low, quad, [owned_tile(4 * quad), owned_tile(4 * quad + 2)])
    contract = (((1,), (1,)), ((), ()))

    def multiply(one, other):
        return lax.dot_general(one, other, contract, preferred_element_type=jnp.float32)

    high, low = all_high[...], all_low[...]
    a_high, a_low = own_high[...], own_low[...]
    partial = multiply(a_high, high) + multiply(a_high, low) + multiply(a_low, high)
    partial = partial * scale
    count = partial.shape[0]
    pieces = total // BLOCK
    for piece in range(pieces):
        partial_ref[pl.ds(piece, count, stride=pieces), :] = partial[
            :, piece * BLOCK : (piece + 1) * BLOCK
        ]
    keep.wait()


def sum_kernel(received_ref, row_ref):
    tiles = received_ref.shape[0] // 8
    sums = [received_ref[at * 8 : (at + 1) * 8, :] for at in range(4)]
    for at in range(4, tiles):
        sums[at % 4] = sums[at % 4] + received_ref[at * 8 : (at + 1) * 8, :]
    total = (sums[0] + sums[1]) + (sums[2] + sums[3])
    row_ref[...] = total[:4, :] + total[4:, :]


def on_device(vectors, tile_table, offsets, tile_ids, bounds):
    vecs, local_rows = vectors.shape
    count = local_rows // BLOCK
    extent = count + 2 * HALO
    edge = HALO * BLOCK
    size = lax.axis_size(ROWS)
    mates = [(i, i ^ 1) for i in range(size)]
    across = [(i, i + 1 if i % 2 else i - 1) for i in range(1, size - 1)]
    vmem = pl.BlockSpec(memory_space=pltpu.VMEM)
    smem = pl.BlockSpec(memory_space=pltpu.SMEM)
    hbm = pl.BlockSpec(memory_space=pltpu.HBM)
    packed = jax.ShapeDtypeStruct((vecs, edge + BLOCK), jnp.float32)
    slots = pltpu.VMEM((3, count), jnp.int32)
    to_mate, to_cross, meta = pl.pallas_call(
        pack_kernel,
        out_shape=(packed, packed, jax.ShapeDtypeStruct((8, BLOCK), jnp.float32)),
        in_specs=[hbm, hbm, hbm],
        out_specs=(vmem, vmem, vmem),
        scratch_shapes=[slots, slots, pltpu.SemaphoreType.DMA((4,))],
        compiler_params=pltpu.CompilerParams(vmem_limit_bytes=4 * MIB),
        name="pack",
    )(*(
        pltpu.with_memory_space_constraint(array, pltpu.HBM)
        for array in (vectors, offsets.T, tile_ids.T)
    ))
    cross = lax.ppermute(to_cross, ROWS, across)
    mate = lax.ppermute(to_mate, ROWS, mates)

    table = pl.pallas_call(
        table_kernel,
        out_shape=jax.ShapeDtypeStruct((3 * NT, BLOCK, 2 * BLOCK), jnp.bfloat16),
        in_specs=[hbm],
        out_specs=vmem,
        scratch_shapes=[
            pltpu.VMEM(tile_table.shape, jnp.float32),
            pltpu.SemaphoreType.DMA((4,)),
        ],
        compiler_params=pltpu.CompilerParams(vmem_limit_bytes=16 * MIB),
        name="table",
    )(pltpu.with_memory_space_constraint(tile_table, pltpu.HBM))

    field = pltpu.VMEM((extent, vecs, BLOCK), jnp.float32)
    parts = pltpu.VMEM((extent, 2 * vecs, BLOCK), jnp.bfloat16)
    filtered, outgoing = pl.pallas_call(
        filter_kernel,
        out_shape=(
            pltpu.VMEM((vecs, local_rows), jnp.float32),
            jax.ShapeDtypeStruct((64, vecs, 2 * BLOCK), jnp.float32),
        ),
        in_specs=[vmem, vmem, vmem, vmem, vmem, smem],
        out_specs=(vmem, vmem),
        scratch_shapes=[
            field, field, field, parts, parts,
            pltpu.VMEM((8, BLOCK), jnp.int32),
            pltpu.SMEM((8, BLOCK), jnp.int32),
            pltpu.SemaphoreType.DMA(()),
        ],
        compiler_params=pltpu.CompilerParams(vmem_limit_bytes=16 * MIB),
        name="filter",
    )(vectors, mate, cross, meta, table, bounds)

    stacked = lax.all_to_all(
        outgoing,
        VEC,
        split_axis=0,
        concat_axis=0,
        tiled=True,
        axis_index_groups=[[at ^ FIRST_TURN for at in range(64)]],
    )
    total = 64 * vecs
    stacked = stacked.reshape(total, 2 * BLOCK)
    owned = total // 4
    partial, kept = pl.pallas_call(
        functools.partial(gram_kernel, 1.0 / (local_rows * size)),
        out_shape=(
            jax.ShapeDtypeStruct((owned * (total // BLOCK), BLOCK), jnp.float32),
            jax.ShapeDtypeStruct(filtered.shape, jnp.float32),
        ),
        in_specs=[vmem, vmem],
        out_specs=(vmem, hbm),
        scratch_shapes=[pltpu.VMEM((total, 2 * BLOCK), jnp.bfloat16)] * 2
        + [pltpu.VMEM((owned, 2 * BLOCK), jnp.bfloat16)] * 2
        + [pltpu.SemaphoreType.DMA(())],
        compiler_params=pltpu.CompilerParams(vmem_limit_bytes=16 * MIB),
        name="gram",
    )(stacked, filtered)
    received = lax.all_to_all(
        partial.reshape(owned, 1, total),
        OWNERS,
        split_axis=0,
        concat_axis=0,
        tiled=True,
        axis_index_groups=[[at ^ SECOND_TURN for at in range(owned)]],
    )
    gram_matrix = pl.pallas_call(
        sum_kernel,
        out_shape=jax.ShapeDtypeStruct((total // BLOCK, BLOCK), jnp.float32),
        in_specs=[vmem],
        out_specs=vmem,
        compiler_params=pltpu.CompilerParams(vmem_limit_bytes=4 * MIB),
        name="sum",
    )(received.reshape(owned * (total // BLOCK), BLOCK)).reshape(1, total)
    return kept, gram_matrix


def solution(mesh):
    fine = Mesh(mesh.devices.reshape(4, 2, 4, 4, 2, 2), ROWS + VEC)
    placed = (P(VEC, ROWS), P(), P(ROWS, None), P(ROWS, None), P())
    return jax.shard_map(
        on_device,
        mesh=fine,
        in_specs=placed,
        out_specs=(P(VEC, ROWS), P(ROWS + VEC, None)),
        check_vma=False,
    )
```

```python
import functools

import jax
import jax.numpy as jnp
from jax import lax
from jax.experimental import pallas as pl
from jax.experimental.pallas import tpu as pltpu
from jax.sharding import Mesh, PartitionSpec as P


BLOCK = 128
STEPS = 4
REACH = 2
HALO = STEPS * REACH
NT = 16
MIB = 1 << 20
ROWS = ("zl", "core")
VEC = ("x", "yq", "yb", "zh")
OWNERS = ROWS + ("x", "yb", "zh")
FIRST_TURN = 0b101011
SECOND_TURN = 0b1111001


def split(value):
    high = value.astype(jnp.bfloat16).astype(jnp.float32)
    return high, value - high


def table_kernel(tiles_ref, table_ref, tiles_here, sems):
    step = NT // sems.shape[0]
    copies = [
        pltpu.make_async_copy(
            tiles_ref.at[at : at + step], tiles_here.at[at : at + step], sems.at[at // step]
        )
        for at in range(0, NT, step)
    ]
    for copy in copies:
        copy.start()
    for tile in range(NT):
        if tile % step == 0:
            copies[tile // step].wait()
        straight = tiles_here[tile]
        flipped = straight.T
        for kind, matrix in enumerate((flipped, straight, (straight + flipped) / 2)):
            high, low = split(matrix)
            entry = tile + NT * kind
            table_ref[entry, :, :BLOCK] = high.astype(jnp.bfloat16)
            table_ref[entry, :, BLOCK:] = low.astype(jnp.bfloat16)


def pack_kernel(
    vectors_ref, offsets_ref, ids_ref, mate_ref, cross_ref, own_ref, offsets_here, ids_here, sems
):
    edge = mate_ref.shape[1] - BLOCK
    last = vectors_ref.shape[1] - edge
    core = lax.axis_index("core")
    to_mate = pl.ds(pl.multiple_of((1 - core) * last, BLOCK), edge)
    to_cross = pl.ds(pl.multiple_of(core * last, BLOCK), edge)
    slots, count = offsets_ref.shape
    copies = [
        pltpu.make_async_copy(source, target, sems.at[at])
        for at, (source, target) in enumerate(
            (
                (offsets_ref, offsets_here),
                (ids_ref, ids_here),
                (vectors_ref.at[:, to_mate], mate_ref.at[:, :edge]),
                (vectors_ref.at[:, to_cross], cross_ref.at[:, :edge]),
            )
        )
    ]
    for copy in copies:
        copy.start()
    own_ref[...] = jnp.zeros_like(own_ref)
    copies[0].wait()
    copies[1].wait()
    own_ref[:slots, :count] = offsets_here[...].astype(jnp.float32)
    own_ref[slots : 2 * slots, :count] = ids_here[...].astype(jnp.float32)
    mate_ref[:, edge:] = own_ref[...]
    cross_ref[:, edge:] = own_ref[...]
    copies[2].wait()
    copies[3].wait()


def filter_kernel(
    vectors_ref, mate_ref, cross_ref, own_ref, table_ref, bounds_ref,
    filtered_ref, outgoing_ref,
    field_a, field_b, field_c, parts_a, parts_b, plan_vector, plan, sem,
):
    vecs = vectors_ref.shape[0]
    count = vectors_ref.shape[1] // BLOCK
    extent = count + 2 * HALO
    edge = HALO * BLOCK

    upper = lax.axis_index("core") == 1

    def before(at):
        return jnp.where(upper, mate_ref[:, at], cross_ref[:, at])

    def after(at):
        return jnp.where(upper, cross_ref[:, at], mate_ref[:, at])

    last = slice(edge, edge + BLOCK)
    lane = lax.broadcasted_iota(jnp.int32, (8, 128), 1)
    row = lax.broadcasted_iota(jnp.int32, (8, 128), 0)
    left = pltpu.roll(before(last), 128 - (count - HALO), 1)
    own = pltpu.roll(own_ref[...], HALO, 1)
    right = pltpu.roll(after(last), HALO + count, 1)
    meta = jnp.where(lane < HALO, left, jnp.where(lane < HALO + count, own, right))
    meta = meta.astype(jnp.int32)
    shift = pltpu.roll(meta, 3, 0)
    kind = jnp.where(shift > 0, 0, jnp.where(shift < 0, NT, 2 * NT))
    plan_vector[...] = jnp.where(row < 3, meta + lane, meta + kind)
    copy = pltpu.make_async_copy(plan_vector, plan, sem)
    copy.start()

    def store_parts(target, block, value):
        high, low = split(value)
        target[block] = jnp.concatenate([high, low], axis=0).astype(jnp.bfloat16)

    for block in range(extent):
        if block < HALO:
            value = before(slice(block * BLOCK, (block + 1) * BLOCK))
        elif block < HALO + count:
            at = (block - HALO) * BLOCK
            value = vectors_ref[:, at : at + BLOCK]
        else:
            at = (block - HALO - count) * BLOCK
            value = after(slice(at, at + BLOCK))
        field_a[block] = value
        store_parts(parts_a, block, value)

    lowest, low_end, high_end = bounds_ref[0], bounds_ref[1], bounds_ref[2]

    def spread(value):
        return jnp.full((vecs, BLOCK), value, jnp.float32)

    half_width = spread((high_end - low_end) * 0.5)
    centre = spread((high_end + low_end) * 0.5)
    sigma_one = half_width / (spread(lowest) - centre)
    sigma_base = 2 / sigma_one
    copy.wait()

    def product(parts, block):
        left_parts, right_parts = [], []
        for slot in range(3):
            left_parts.append(parts[plan[slot, block]])
            right_parts.append(table_ref[plan[3 + slot, block]])
        both = lax.dot_general(
            jnp.concatenate(left_parts, axis=1),
            jnp.concatenate(right_parts, axis=0),
            (((1,), (0,)), ((), ())),
            preferred_element_type=jnp.float32,
        )
        return both[:vecs, :BLOCK] + both[vecs:, :BLOCK] + both[:vecs, BLOCK:]

    fields = [field_a, field_b, field_c, field_a]
    parts = [parts_a, parts_b, parts_a, parts_b]
    sigma = sigma_one
    for step in range(1, STEPS + 1):
        source, source_parts = fields[step - 1], parts[step - 1]
        if step == 1:
            scale, drag = sigma_one / half_width, None
        else:
            following = 1 / (sigma_base - sigma)
            scale, drag = 2 * following / half_width, sigma * following
            sigma = following
        first = REACH * step

        def one_block(block, owner, part):
            value = scale * (product(source_parts, block) - centre * source[block])
            if drag is not None:
                value = value - drag * fields[step - 2][block]
            if step < STEPS:
                fields[step][block] = value
                store_parts(parts[step], block, value)
            else:
                at = block - HALO
                filtered_ref[:, pl.ds(pl.multiple_of(at * BLOCK, BLOCK), BLOCK)] = value
                upper, lower = owner
                for quarter in range(4):
                    inner = (lower // 4 * 16 + quarter * 4 + lower % 4) ^ (FIRST_TURN % 32)
                    outgoing_ref[
                        (upper ^ (FIRST_TURN // 32)) * 32 + inner,
                        :,
                        part * BLOCK : (part + 1) * BLOCK,
                    ] = value

        group = (extent - 2 * first) // 2

        @pl.loop(0, 2)
        def _(index):
            for inner in range(group):
                one_block(first + index * group + inner, (index, inner // 2), inner % 2)


def gram_kernel(
    scale, stacked_ref, partial_ref, all_high, all_low, own_high, own_low
):
    total = stacked_ref.shape[0]
    quarter = lax.axis_index("yq")

    def arrived(at):
        return stacked_ref[pl.ds(pl.multiple_of((at ^ FIRST_TURN) * 8, 8), 8), :]

    def store(high_ref, low_ref, at, tiles):
        high, low = split(jnp.concatenate(tiles, axis=0))
        high_ref[at * 16 : (at + 1) * 16, :] = high.astype(jnp.bfloat16)
        low_ref[at * 16 : (at + 1) * 16, :] = low.astype(jnp.bfloat16)

    for pair in range(total // 16):
        store(all_high, all_low, pair, [arrived(2 * pair), arrived(2 * pair + 1)])

    upper_rows = lax.broadcasted_iota(jnp.int32, (8, stacked_ref.shape[1]), 0) < 4
    odd = quarter % 2 == 1

    row = lax.broadcasted_iota(jnp.int32, (8, stacked_ref.shape[1]), 0)

    def turned_rows(tile):
        for bit in (1, 2):
            if SECOND_TURN & bit:
                back, forth = pltpu.roll(tile, 8 - bit, 0), pltpu.roll(tile, bit, 0)
                tile = jnp.where(row & bit == 0, back, forth)
        return tile

    def owned_tile(at):
        tiles = [arrived((slot ^ (SECOND_TURN // 4)) * 2 + quarter // 2) for slot in (at, at + 1)]
        turned = [pltpu.roll(tile, 4, 0) for tile in tiles]
        first = jnp.where(odd, turned[0], tiles[0])
        second = jnp.where(odd, tiles[1], turned[1])
        return turned_rows(jnp.where(upper_rows, first, second))

    for quad in range(8):
        store(own_high, own_low, quad, [owned_tile(4 * quad), owned_tile(4 * quad + 2)])
    contract = (((1,), (1,)), ((), ()))

    def multiply(one, other):
        return lax.dot_general(one, other, contract, preferred_element_type=jnp.float32)

    high, low = all_high[...], all_low[...]
    a_high, a_low = own_high[...], own_low[...]
    partial = multiply(a_high, high) + multiply(a_high, low) + multiply(a_low, high)
    partial = partial * scale
    count = partial.shape[0]
    pieces = total // BLOCK
    for piece in range(pieces):
        partial_ref[pl.ds(piece, count, stride=pieces), :] = partial[
            :, piece * BLOCK : (piece + 1) * BLOCK
        ]


def sum_kernel(received_ref, filtered_ref, row_ref, kept_ref, sem):
    keep = pltpu.make_async_copy(filtered_ref, kept_ref, sem)
    keep.start()
    tiles = received_ref.shape[0] // 8
    sums = [received_ref[at * 8 : (at + 1) * 8, :] for at in range(4)]
    for at in range(4, tiles):
        sums[at % 4] = sums[at % 4] + received_ref[at * 8 : (at + 1) * 8, :]
    total = (sums[0] + sums[1]) + (sums[2] + sums[3])
    row_ref[...] = total[:4, :] + total[4:, :]
    keep.wait()


def on_device(vectors, tile_table, offsets, tile_ids, bounds):
    vecs, local_rows = vectors.shape
    count = local_rows // BLOCK
    extent = count + 2 * HALO
    edge = HALO * BLOCK
    size = lax.axis_size(ROWS)
    mates = [(i, i ^ 1) for i in range(size)]
    across = [(i, i + 1 if i % 2 else i - 1) for i in range(1, size - 1)]
    vmem = pl.BlockSpec(memory_space=pltpu.VMEM)
    smem = pl.BlockSpec(memory_space=pltpu.SMEM)
    hbm = pl.BlockSpec(memory_space=pltpu.HBM)
    packed = jax.ShapeDtypeStruct((vecs, edge + BLOCK), jnp.float32)
    slots = pltpu.VMEM((3, count), jnp.int32)
    to_mate, to_cross, meta = pl.pallas_call(
        pack_kernel,
        out_shape=(packed, packed, jax.ShapeDtypeStruct((8, BLOCK), jnp.float32)),
        in_specs=[hbm, hbm, hbm],
        out_specs=(vmem, vmem, vmem),
        scratch_shapes=[slots, slots, pltpu.SemaphoreType.DMA((4,))],
        compiler_params=pltpu.CompilerParams(vmem_limit_bytes=4 * MIB),
        name="pack",
    )(*(
        pltpu.with_memory_space_constraint(array, pltpu.HBM)
        for array in (vectors, offsets.T, tile_ids.T)
    ))
    cross = lax.ppermute(to_cross, ROWS, across)
    mate = lax.ppermute(to_mate, ROWS, mates)

    table = pl.pallas_call(
        table_kernel,
        out_shape=jax.ShapeDtypeStruct((3 * NT, BLOCK, 2 * BLOCK), jnp.bfloat16),
        in_specs=[hbm],
        out_specs=vmem,
        scratch_shapes=[
            pltpu.VMEM(tile_table.shape, jnp.float32),
            pltpu.SemaphoreType.DMA((NT,)),
        ],
        compiler_params=pltpu.CompilerParams(vmem_limit_bytes=16 * MIB),
        name="table",
    )(pltpu.with_memory_space_constraint(tile_table, pltpu.HBM))

    field = pltpu.VMEM((extent, vecs, BLOCK), jnp.float32)
    parts = pltpu.VMEM((extent, 2 * vecs, BLOCK), jnp.bfloat16)
    filtered, outgoing = pl.pallas_call(
        filter_kernel,
        out_shape=(
            pltpu.VMEM((vecs, local_rows), jnp.float32),
            jax.ShapeDtypeStruct((64, vecs, 2 * BLOCK), jnp.float32),
        ),
        in_specs=[vmem, vmem, vmem, vmem, vmem, smem],
        out_specs=(vmem, vmem),
        scratch_shapes=[
            field, field, field, parts, parts,
            pltpu.VMEM((8, BLOCK), jnp.int32),
            pltpu.SMEM((8, BLOCK), jnp.int32),
            pltpu.SemaphoreType.DMA(()),
        ],
        compiler_params=pltpu.CompilerParams(vmem_limit_bytes=16 * MIB),
        name="filter",
    )(vectors, mate, cross, meta, table, bounds)

    stacked = lax.all_to_all(
        outgoing,
        VEC,
        split_axis=0,
        concat_axis=0,
        tiled=True,
        axis_index_groups=[[at ^ FIRST_TURN for at in range(64)]],
    )
    total = 64 * vecs
    stacked = stacked.reshape(total, 2 * BLOCK)
    owned = total // 4
    partial = pl.pallas_call(
        functools.partial(gram_kernel, 1.0 / (local_rows * size)),
        out_shape=jax.ShapeDtypeStruct((owned * (total // BLOCK), BLOCK), jnp.float32),
        in_specs=[vmem],
        out_specs=vmem,
        scratch_shapes=[pltpu.VMEM((total, 2 * BLOCK), jnp.bfloat16)] * 2
        + [pltpu.VMEM((owned, 2 * BLOCK), jnp.bfloat16)] * 2,
        compiler_params=pltpu.CompilerParams(vmem_limit_bytes=16 * MIB),
        name="gram",
    )(stacked)
    received = lax.all_to_all(
        partial.reshape(owned, 1, total),
        OWNERS,
        split_axis=0,
        concat_axis=0,
        tiled=True,
        axis_index_groups=[[at ^ SECOND_TURN for at in range(owned)]],
    )
    row, kept = pl.pallas_call(
        sum_kernel,
        out_shape=(
            jax.ShapeDtypeStruct((total // BLOCK, BLOCK), jnp.float32),
            jax.ShapeDtypeStruct(filtered.shape, jnp.float32),
        ),
        in_specs=[vmem, vmem],
        out_specs=(vmem, hbm),
        scratch_shapes=[pltpu.SemaphoreType.DMA(())],
        compiler_params=pltpu.CompilerParams(vmem_limit_bytes=4 * MIB),
        name="sum",
    )(received.reshape(owned * (total // BLOCK), BLOCK), filtered)
    return kept, row.reshape(1, total)


def solution(mesh):
    fine = Mesh(mesh.devices.reshape(4, 2, 4, 4, 2, 2), ROWS + VEC)
    placed = (P(VEC, ROWS), P(), P(ROWS, None), P(ROWS, None), P())
    return jax.shard_map(
        on_device,
        mesh=fine,
        in_specs=placed,
        out_specs=(P(VEC, ROWS), P(ROWS + VEC, None)),
        check_vma=False,
    )
```

```python
import functools

import jax
import jax.numpy as jnp
from jax import lax
from jax.experimental import pallas as pl
from jax.experimental.pallas import tpu as pltpu
from jax.sharding import Mesh, PartitionSpec as P


BLOCK = 128
STEPS = 4
REACH = 2
HALO = STEPS * REACH
NT = 16
MIB = 1 << 20
ROWS = ("zl", "core")
VEC = ("x", "yq", "yb", "zh")
OWNERS = ROWS + ("x", "yb", "zh")
FIRST_TURN = 0b101011
SECOND_TURN = 0b0111001


def split(value):
    high = value.astype(jnp.bfloat16).astype(jnp.float32)
    return high, value - high


def table_kernel(tiles_ref, table_ref, tiles_here, sems):
    step = NT // sems.shape[0]
    copies = [
        pltpu.make_async_copy(
            tiles_ref.at[at : at + step], tiles_here.at[at : at + step], sems.at[at // step]
        )
        for at in range(0, NT, step)
    ]
    for copy in copies:
        copy.start()
    for tile in range(NT):
        if tile % step == 0:
            copies[tile // step].wait()
        straight = tiles_here[tile]
        flipped = straight.T
        for kind, matrix in enumerate((flipped, straight, (straight + flipped) / 2)):
            high, low = split(matrix)
            entry = tile + NT * kind
            table_ref[entry, :, :BLOCK] = high.astype(jnp.bfloat16)
            table_ref[entry, :, BLOCK:] = low.astype(jnp.bfloat16)


def pack_kernel(
    vectors_ref, offsets_ref, ids_ref, mate_ref, cross_ref, own_ref, offsets_here, ids_here, sems
):
    edge = mate_ref.shape[1] - BLOCK
    last = vectors_ref.shape[1] - edge
    core = lax.axis_index("core")
    to_mate = pl.ds(pl.multiple_of((1 - core) * last, BLOCK), edge)
    to_cross = pl.ds(pl.multiple_of(core * last, BLOCK), edge)
    slots, count = offsets_ref.shape
    copies = [
        pltpu.make_async_copy(source, target, sems.at[at])
        for at, (source, target) in enumerate(
            (
                (offsets_ref, offsets_here),
                (ids_ref, ids_here),
                (vectors_ref.at[:, to_mate], mate_ref.at[:, :edge]),
                (vectors_ref.at[:, to_cross], cross_ref.at[:, :edge]),
            )
        )
    ]
    for copy in copies:
        copy.start()
    own_ref[...] = jnp.zeros_like(own_ref)
    copies[0].wait()
    copies[1].wait()
    own_ref[:slots, :count] = offsets_here[...].astype(jnp.float32)
    own_ref[slots : 2 * slots, :count] = ids_here[...].astype(jnp.float32)
    mate_ref[:, edge:] = own_ref[...]
    cross_ref[:, edge:] = own_ref[...]
    copies[2].wait()
    copies[3].wait()


def filter_kernel(
    vectors_ref, mate_ref, cross_ref, own_ref, table_ref, bounds_ref,
    filtered_ref, outgoing_ref,
    field_a, field_b, field_c, parts_a, parts_b, plan_vector, plan, sem,
):
    vecs = vectors_ref.shape[0]
    count = vectors_ref.shape[1] // BLOCK
    extent = count + 2 * HALO
    edge = HALO * BLOCK

    upper = lax.axis_index("core") == 1

    def before(at):
        return jnp.where(upper, mate_ref[:, at], cross_ref[:, at])

    def after(at):
        return jnp.where(upper, cross_ref[:, at], mate_ref[:, at])

    last = slice(edge, edge + BLOCK)
    lane = lax.broadcasted_iota(jnp.int32, (8, 128), 1)
    row = lax.broadcasted_iota(jnp.int32, (8, 128), 0)
    left = pltpu.roll(before(last), 128 - (count - HALO), 1)
    own = pltpu.roll(own_ref[...], HALO, 1)
    right = pltpu.roll(after(last), HALO + count, 1)
    meta = jnp.where(lane < HALO, left, jnp.where(lane < HALO + count, own, right))
    meta = meta.astype(jnp.int32)
    shift = pltpu.roll(meta, 3, 0)
    kind = jnp.where(shift > 0, 0, jnp.where(shift < 0, NT, 2 * NT))
    plan_vector[...] = jnp.where(row < 3, meta + lane, meta + kind)
    copy = pltpu.make_async_copy(plan_vector, plan, sem)
    copy.start()

    def store_parts(target, block, value):
        high, low = split(value)
        target[block] = jnp.concatenate([high, low], axis=0).astype(jnp.bfloat16)

    for block in range(extent):
        if block < HALO:
            value = before(slice(block * BLOCK, (block + 1) * BLOCK))
        elif block < HALO + count:
            at = (block - HALO) * BLOCK
            value = vectors_ref[:, at : at + BLOCK]
        else:
            at = (block - HALO - count) * BLOCK
            value = after(slice(at, at + BLOCK))
        field_a[block] = value
        store_parts(parts_a, block, value)

    lowest, low_end, high_end = bounds_ref[0], bounds_ref[1], bounds_ref[2]

    def spread(value):
        return jnp.full((vecs, BLOCK), value, jnp.float32)

    half_width = spread((high_end - low_end) * 0.5)
    centre = spread((high_end + low_end) * 0.5)
    sigma_one = half_width / (spread(lowest) - centre)
    sigma_base = 2 / sigma_one
    copy.wait()

    def product(parts, block):
        left_parts, right_parts = [], []
        for slot in range(3):
            left_parts.append(parts[plan[slot, block]])
            right_parts.append(table_ref[plan[3 + slot, block]])
        both = lax.dot_general(
            jnp.concatenate(left_parts, axis=1),
            jnp.concatenate(right_parts, axis=0),
            (((1,), (0,)), ((), ())),
            preferred_element_type=jnp.float32,
        )
        return both[:vecs, :BLOCK] + both[vecs:, :BLOCK] + both[:vecs, BLOCK:]

    fields = [field_a, field_b, field_c, field_a]
    parts = [parts_a, parts_b, parts_a, parts_b]
    sigma = sigma_one
    for step in range(1, STEPS + 1):
        source, source_parts = fields[step - 1], parts[step - 1]
        if step == 1:
            scale, drag = sigma_one / half_width, None
        else:
            following = 1 / (sigma_base - sigma)
            scale, drag = 2 * following / half_width, sigma * following
            sigma = following
        first = REACH * step

        def one_block(block, owner, part):
            value = scale * (product(source_parts, block) - centre * source[block])
            if drag is not None:
                value = value - drag * fields[step - 2][block]
            if step < STEPS:
                fields[step][block] = value
                store_parts(parts[step], block, value)
            else:
                at = block - HALO
                filtered_ref[:, at * BLOCK : (at + 1) * BLOCK] = value
                upper, lower = owner
                for quarter in range(4):
                    inner = (lower // 4 * 16 + quarter * 4 + lower % 4) ^ (FIRST_TURN % 32)
                    outgoing_ref[
                        (upper ^ (FIRST_TURN // 32)) * 32 + inner,
                        :,
                        part * BLOCK : (part + 1) * BLOCK,
                    ] = value

        for inner in range(extent - 2 * first):
            one_block(first + inner, divmod(inner // 2, count // 4), inner % 2)


def gram_kernel(
    scale, stacked_ref, filtered_ref, partial_ref, kept_ref,
    all_high, all_low, own_high, own_low, sem,
):
    keep = pltpu.make_async_copy(filtered_ref, kept_ref, sem)
    keep.start()
    total = stacked_ref.shape[0]
    quarter = lax.axis_index("yq")

    def arrived(at):
        return stacked_ref[pl.ds(pl.multiple_of((at ^ FIRST_TURN) * 8, 8), 8), :]

    def store(high_ref, low_ref, at, tiles):
        high, low = split(jnp.concatenate(tiles, axis=0))
        high_ref[at * 16 : (at + 1) * 16, :] = high.astype(jnp.bfloat16)
        low_ref[at * 16 : (at + 1) * 16, :] = low.astype(jnp.bfloat16)

    for pair in range(total // 16):
        store(all_high, all_low, pair, [arrived(2 * pair), arrived(2 * pair + 1)])

    upper_rows = lax.broadcasted_iota(jnp.int32, (8, stacked_ref.shape[1]), 0) < 4
    odd = quarter % 2 == 1

    row = lax.broadcasted_iota(jnp.int32, (8, stacked_ref.shape[1]), 0)

    def turned_rows(tile):
        for bit in (1, 2):
            if SECOND_TURN & bit:
                back, forth = pltpu.roll(tile, 8 - bit, 0), pltpu.roll(tile, bit, 0)
                tile = jnp.where(row & bit == 0, back, forth)
        return tile

    def owned_tile(at):
        tiles = [arrived((slot ^ (SECOND_TURN // 4)) * 2 + quarter // 2) for slot in (at, at + 1)]
        turned = [pltpu.roll(tile, 4, 0) for tile in tiles]
        first = jnp.where(odd, turned[0], tiles[0])
        second = jnp.where(odd, tiles[1], turned[1])
        return turned_rows(jnp.where(upper_rows, first, second))

    for quad in range(8):
        store(own_high, own_low, quad, [owned_tile(4 * quad), owned_tile(4 * quad + 2)])
    contract = (((1,), (1,)), ((), ()))

    def multiply(one, other):
        return lax.dot_general(one, other, contract, preferred_element_type=jnp.float32)

    high, low = all_high[...], all_low[...]
    a_high, a_low = own_high[...], own_low[...]
    partial = multiply(a_high, high) + multiply(a_high, low) + multiply(a_low, high)
    partial = partial * scale
    count = partial.shape[0]
    pieces = total // BLOCK
    for piece in range(pieces):
        partial_ref[pl.ds(piece, count, stride=pieces), :] = partial[
            :, piece * BLOCK : (piece + 1) * BLOCK
        ]
    keep.wait()


def sum_kernel(received_ref, row_ref):
    tiles = received_ref.shape[0] // 8
    sums = [received_ref[at * 8 : (at + 1) * 8, :] for at in range(4)]
    for at in range(4, tiles):
        sums[at % 4] = sums[at % 4] + received_ref[at * 8 : (at + 1) * 8, :]
    total = (sums[0] + sums[1]) + (sums[2] + sums[3])
    row_ref[...] = total[:4, :] + total[4:, :]


def on_device(vectors, tile_table, offsets, tile_ids, bounds):
    vecs, local_rows = vectors.shape
    count = local_rows // BLOCK
    extent = count + 2 * HALO
    edge = HALO * BLOCK
    size = lax.axis_size(ROWS)
    mates = [(i, i ^ 1) for i in range(size)]
    across = [(i, i + 1 if i % 2 else i - 1) for i in range(1, size - 1)]
    vmem = pl.BlockSpec(memory_space=pltpu.VMEM)
    smem = pl.BlockSpec(memory_space=pltpu.SMEM)
    hbm = pl.BlockSpec(memory_space=pltpu.HBM)
    packed = jax.ShapeDtypeStruct((vecs, edge + BLOCK), jnp.float32)
    slots = pltpu.VMEM((3, count), jnp.int32)
    to_mate, to_cross, meta = pl.pallas_call(
        pack_kernel,
        out_shape=(packed, packed, jax.ShapeDtypeStruct((8, BLOCK), jnp.float32)),
        in_specs=[hbm, hbm, hbm],
        out_specs=(vmem, vmem, vmem),
        scratch_shapes=[slots, slots, pltpu.SemaphoreType.DMA((4,))],
        compiler_params=pltpu.CompilerParams(vmem_limit_bytes=4 * MIB),
        name="pack",
    )(*(
        pltpu.with_memory_space_constraint(array, pltpu.HBM)
        for array in (vectors, offsets.T, tile_ids.T)
    ))
    cross = lax.ppermute(to_cross, ROWS, across)
    mate = lax.ppermute(to_mate, ROWS, mates)

    table = pl.pallas_call(
        table_kernel,
        out_shape=jax.ShapeDtypeStruct((3 * NT, BLOCK, 2 * BLOCK), jnp.bfloat16),
        in_specs=[hbm],
        out_specs=vmem,
        scratch_shapes=[
            pltpu.VMEM(tile_table.shape, jnp.float32),
            pltpu.SemaphoreType.DMA((4,)),
        ],
        compiler_params=pltpu.CompilerParams(vmem_limit_bytes=16 * MIB),
        name="table",
    )(pltpu.with_memory_space_constraint(tile_table, pltpu.HBM))

    field = pltpu.VMEM((extent, vecs, BLOCK), jnp.float32)
    parts = pltpu.VMEM((extent, 2 * vecs, BLOCK), jnp.bfloat16)
    filtered, outgoing = pl.pallas_call(
        filter_kernel,
        out_shape=(
            pltpu.VMEM((vecs, local_rows), jnp.float32),
            jax.ShapeDtypeStruct((64, vecs, 2 * BLOCK), jnp.float32),
        ),
        in_specs=[vmem, vmem, vmem, vmem, vmem, smem],
        out_specs=(vmem, vmem),
        scratch_shapes=[
            field, field, field, parts, parts,
            pltpu.VMEM((8, BLOCK), jnp.int32),
            pltpu.SMEM((8, BLOCK), jnp.int32),
            pltpu.SemaphoreType.DMA(()),
        ],
        compiler_params=pltpu.CompilerParams(vmem_limit_bytes=16 * MIB),
        name="filter",
    )(vectors, mate, cross, meta, table, bounds)

    stacked = lax.all_to_all(
        outgoing,
        VEC,
        split_axis=0,
        concat_axis=0,
        tiled=True,
        axis_index_groups=[[at ^ FIRST_TURN for at in range(64)]],
    )
    total = 64 * vecs
    stacked = stacked.reshape(total, 2 * BLOCK)
    owned = total // 4
    partial, kept = pl.pallas_call(
        functools.partial(gram_kernel, 1.0 / (local_rows * size)),
        out_shape=(
            jax.ShapeDtypeStruct((owned * (total // BLOCK), BLOCK), jnp.float32),
            jax.ShapeDtypeStruct(filtered.shape, jnp.float32),
        ),
        in_specs=[vmem, vmem],
        out_specs=(vmem, hbm),
        scratch_shapes=[pltpu.VMEM((total, 2 * BLOCK), jnp.bfloat16)] * 2
        + [pltpu.VMEM((owned, 2 * BLOCK), jnp.bfloat16)] * 2
        + [pltpu.SemaphoreType.DMA(())],
        compiler_params=pltpu.CompilerParams(vmem_limit_bytes=16 * MIB),
        name="gram",
    )(stacked, filtered)
    received = lax.all_to_all(
        partial.reshape(owned, 1, total),
        OWNERS,
        split_axis=0,
        concat_axis=0,
        tiled=True,
        axis_index_groups=[[at ^ SECOND_TURN for at in range(owned)]],
    )
    gram_matrix = pl.pallas_call(
        sum_kernel,
        out_shape=jax.ShapeDtypeStruct((total // BLOCK, BLOCK), jnp.float32),
        in_specs=[vmem],
        out_specs=vmem,
        compiler_params=pltpu.CompilerParams(vmem_limit_bytes=4 * MIB),
        name="sum",
    )(received.reshape(owned * (total // BLOCK), BLOCK)).reshape(1, total)
    return kept, gram_matrix


def solution(mesh):
    fine = Mesh(mesh.devices.reshape(4, 2, 4, 4, 2, 2), ROWS + VEC)
    placed = (P(VEC, ROWS), P(), P(ROWS, None), P(ROWS, None), P())
    return jax.shard_map(
        on_device,
        mesh=fine,
        in_specs=placed,
        out_specs=(P(VEC, ROWS), P(ROWS + VEC, None)),
        check_vma=False,
    )
```
